256 devices in a mesh: lon: 64 (over y_hi, x, z), lat: 4 (over y_lo, core).
Axes of the slice: x: 4, y: 4 (y_hi: 2, y_lo: 2; y = y_hi * 2 + y_lo), z: 8, core: 2. Of those that a mesh axis runs over, the one named last changes fastest.
Arguments:
- expanded: bfloat16 [32, 1024, 3072], P('lat', 'lon'), may hold values from -6 to 6
- stream: bfloat16 [32, 1024, 768], P('lat', 'lon'), may hold values from -6 to 6
- land: int32 [32, 1024], P('lat', 'lon'), may hold values 0 or 1
- polar: int32 [32], replicated, may hold values from 0 to 1, as said below
- land_shift: float32 [3072], replicated, may hold values from -4 to 4
- dw_kernel: float32 [3, 3, 3072], replicated, may hold values from -2 to 2
- w_proj: bfloat16 [3072, 768], replicated, may hold values from -0.109375 to 0.109375
- w_qkv: bfloat16 [768, 2304], replicated, may hold values from -0.21875 to 0.21875
- w_out: bfloat16 [768, 768], replicated, may hold values from -0.21875 to 0.21875
- rel_bias: float32 [24, 15, 8], replicated, may hold values from -2 to 250
Outputs:
- mixed_out: bfloat16 [32, 1024, 768], P('lat', 'lon')
The draws below stay inside these ranges and needn't reach their ends.
Inputs may be any that keep to these rules, and one draw needn't show every extreme that they name: `polar`: 1 marks the first a and the last b token rows, 1 <= a, b <= 4, at least one of a, b equal to 4; all other rows are 0.
All inputs are finite; a program needn't handle non-finite values. No bound on the sum of `land` on one device may be relied on, other than what follows from the above.
Results may differ from the reference program's by a relative error of at most 0.0075.
Values may be sent and summed in bfloat16 or wider, within the bound.
No kernel may reach another device: no remote copies, remote signals or barrier semaphores. Data moves between devices by JAX's collectives and lax.ppermute only.
A program may use at most 128 MiB of HBM per device.

```python
import jax
import jax.numpy as jnp
import numpy as np
from jax import lax

D = 768
HEADS = 24
EXP = 3072
GRID = 8
CAP = 4
ROWS = 32
COLS = 1024


def draw_polar(key, part):
    first, second, third = jax.random.split(jax.random.fold_in(key, 11), 3)
    top = jax.random.randint(first, (), 1, CAP + 1)
    bottom = jax.random.randint(second, (), 1, CAP + 1)
    side = jax.random.randint(third, (), 0, 2)
    top = jnp.where(side == 0, CAP, top)
    bottom = jnp.where(side == 1, CAP, bottom)
    rows = jnp.arange(ROWS)
    return ((rows < top) | (rows >= ROWS - bottom)).astype(jnp.int32)


def draw_rel_bias(key, part):
    base_key = jax.random.fold_in(jax.random.fold_in(key, 23), 0)
    table = jax.random.uniform(base_key, (HEADS, 2 * GRID - 1, GRID), jnp.float32, -2.0, 2.0)
    return table.astype(jnp.float32)


def place_ends(drawn, rng, low, largest):
    index_at = [jax.random.randint(jax.random.fold_in(rng, axis), (), 0, length) for axis, length in enumerate(drawn.shape)]
    widest = drawn.shape.index(max(drawn.shape))
    neighbour = index_at[:widest] + [(index_at[widest] + 1) % drawn.shape[widest]] + index_at[widest + 1:]
    return drawn.at[tuple(index_at)].set(low).at[tuple(neighbour)].set(largest)


def steps_of(own_key, shape, cuts, low, largest):
    factor_of = 1.0
    for axis_at, shards_of in cuts:
        heights = jax.random.uniform(jax.random.fold_in(jax.random.fold_in(own_key, 6), axis_at), (shards_of,), jnp.float32, low / len(cuts), largest / len(cuts))
        factor_of = factor_of * jnp.repeat(jnp.exp(heights), shape[axis_at] // shards_of).reshape((-1,) + (1,) * (len(shape) - 1 - axis_at))
    return factor_of


def scatter_about(rng, dims, scale, bound, cuts=(), held_as=jnp.bfloat16):
    values = scale * jax.random.normal(rng, dims, jnp.float32)
    if cuts:
        values = values * steps_of(rng, dims, cuts, -0.22, 0.18)
    return jnp.clip(values, -bound, bound).astype(held_as)


def setup_inputs(seed: int = 0) -> dict:
    key_of = jax.random.split(jax.random.key(seed), 11)
    expanded = scatter_about(key_of[0], (ROWS, COLS, EXP), 1.0, 6.0, ((0, 4), (1, 64)))
    stream = scatter_about(key_of[1], (ROWS, COLS, D), 1.0, 6.0, ((0, 4), (1, 64)))
    land = place_ends((jax.random.randint(key_of[2], (ROWS, COLS), 0, 10) < 3).astype(jnp.int32), jax.random.fold_in(key_of[2], 1), 0, 1)
    polar = draw_polar(jax.random.fold_in(key_of[10], 71), 0)
    land_shift = scatter_about(key_of[4], (EXP,), 1.0, 4.0, (), jnp.float32)
    dw_kernel = scatter_about(key_of[5], (3, 3, EXP), 9 ** -0.5, 2.0, (), jnp.float32)
    w_proj = scatter_about(key_of[6], (EXP, D), EXP ** -0.5, 0.109375)
    w_qkv = scatter_about(key_of[7], (D, 3 * D), D ** -0.5, 0.21875)
    w_out = scatter_about(key_of[8], (D, D), D ** -0.5, 0.21875)
    rel_bias = draw_rel_bias(jax.random.fold_in(key_of[10], 71), 0)
    return {"expanded": expanded, "stream": stream, "land": land, "polar": polar, "land_shift": land_shift, "dw_kernel": dw_kernel, "w_proj": w_proj, "w_qkv": w_qkv, "w_out": w_out, "rel_bias": rel_bias}


eps = 1e-05

def reference(expanded, stream, land, polar, land_shift, dw_kernel, w_proj, w_qkv, w_out, rel_bias):
    rows_all, cols_all, width_exp = expanded.shape
    width = stream.shape[2]
    heads = rel_bias.shape[0]
    head_dim = width // heads
    padded = jnp.pad(expanded, ((1, 1), (0, 0), (0, 0)))
    padded = jnp.concatenate([padded[:, -1:], padded, padded[:, :1]], axis=1)

    def mix_row(index):
        band = lax.dynamic_slice_in_dim(padded, index, 3, 0).astype(jnp.float32)
        land_row = lax.dynamic_index_in_dim(land, index, 0, keepdims=False)
        filtered = land_row[:, None].astype(jnp.float32) * land_shift[None, :]
        for row_tap in range(3):
            for col_tap in range(3):
                filtered = filtered + band[row_tap, col_tap:col_tap + cols_all] * dw_kernel[row_tap, col_tap]
        activated = jax.nn.gelu(filtered).astype(jnp.bfloat16)
        base = lax.dynamic_index_in_dim(stream, index, 0, keepdims=False).astype(jnp.float32)
        return (base + jnp.dot(activated, w_proj, preferred_element_type=jnp.float32)).astype(jnp.bfloat16)
    mixed = lax.map(mix_row, jnp.arange(rows_all, dtype=jnp.int32))
    flat = mixed.reshape(-1, width).astype(jnp.float32)
    centre = lax.optimization_barrier(jnp.mean(flat, axis=1, keepdims=True))
    centred = flat - centre
    spread = lax.optimization_barrier(jnp.mean(centred * centred, axis=1, keepdims=True))
    normed = (centred * lax.rsqrt(spread + eps)).astype(jnp.bfloat16)
    qkv = jnp.dot(normed, w_qkv, preferred_element_type=jnp.float32).astype(jnp.bfloat16)
    strip = rows_all // GRID
    band_cols = cols_all // GRID

    def split(block):
        return block.reshape(GRID, strip, GRID, band_cols, heads, head_dim)
    queries = split(qkv[:, :width])
    keys = split(qkv[:, width:2 * width])
    values = split(qkv[:, 2 * width:])
    lat_query = np.arange(GRID)[:, None, None, None]
    lon_query = np.arange(GRID)[None, :, None, None]
    lat_key = np.arange(GRID)[None, None, :, None]
    lon_key = np.arange(GRID)[None, None, None, :]
    lat_index = lat_key - lat_query + GRID - 1 + 0 * lon_key + 0 * lon_query
    lon_index = (lon_key - lon_query) % GRID + 0 * lat_key + 0 * lat_query
    table = rel_bias[:, lat_index, lon_index]
    cap_rows = polar.reshape(GRID, strip)

    def attend_strip(index):
        query_part = lax.dynamic_index_in_dim(queries, index, 1, keepdims=False).astype(jnp.float32)
        key_part = lax.dynamic_index_in_dim(keys, index, 1, keepdims=False).astype(jnp.float32)
        value_part = lax.dynamic_index_in_dim(values, index, 1, keepdims=False).astype(jnp.float32)
        allowed = lax.dynamic_index_in_dim(cap_rows, index, 1, keepdims=False) == 0
        scores = jnp.einsum('mnchd,kjchd->chmnkj', query_part, key_part) * head_dim ** (-0.5) + table[None]
        scores = jnp.where(allowed[None, None, None, None, :, None], scores, -1e+30)
        shape_full = scores.shape
        scores = scores.reshape(shape_full[:4] + (GRID * GRID,))
        peak = lax.optimization_barrier(jnp.max(scores, axis=-1, keepdims=True))
        weights = jnp.exp(scores - peak)
        probs = (weights / lax.optimization_barrier(jnp.sum(weights, axis=-1, keepdims=True))).astype(jnp.bfloat16)
        probs = probs.reshape(shape_full).astype(jnp.float32)
        attended = jnp.einsum('chmnkj,kjchd->mnchd', probs, value_part)
        return attended.astype(jnp.bfloat16)
    pieces = lax.map(attend_strip, jnp.arange(strip, dtype=jnp.int32))
    attended = jnp.transpose(pieces, (1, 0, 2, 3, 4, 5)).reshape(rows_all * cols_all, width)
    result = flat.astype(jnp.float32) + jnp.dot(attended, w_out, preferred_element_type=jnp.float32)
    return result.astype(jnp.bfloat16).reshape(rows_all, cols_all, width)
```

```python
import functools

import jax
import jax.numpy as jnp
import numpy as np
from jax import lax
from jax.experimental import pallas as pl
from jax.experimental.pallas import tpu as pltpu
from jax.sharding import Mesh
from jax.sharding import PartitionSpec as P

GRID = 8
EPS = 1e-05
NEG = -1e30
F32 = jnp.float32
BF16 = jnp.bfloat16
VM = pl.BlockSpec(memory_space=pltpu.VMEM)
SM = pl.BlockSpec(memory_space=pltpu.SMEM)
HBM = pl.BlockSpec(memory_space=pl.ANY)


def send_order(rows, cols):
    strips = rows // 2
    order = []
    for s in range(strips):
        for c2 in range(cols // 2):
            for m in range(2):
                for c1 in range(2):
                    order.append((m * strips + s) * cols + 2 * c2 + c1)
    return np.array(order)


def pack_columns(flags, e_ref, ra_ref, rb_ref, ca_ref, cb_ref, first, last):
    lat_even = flags[0] == 1
    lon_even = flags[1] == 1
    rows, cols, _ = e_ref.shape
    ra = ra_ref[...].astype(F32)
    rb = rb_ref[...].astype(F32)
    top = jnp.where(lat_even, rb, ra)
    bottom = jnp.where(lat_even, ra, rb)
    for r in range(rows + 2):
        line = top if r == 0 else bottom if r == rows + 1 else e_ref[r - 1].astype(F32)
        first[r : r + 1, :] = line[0:1]
        last[r : r + 1, :] = line[cols - 1 : cols]
    a = jnp.where(lon_even, last[...], first[...])
    b = jnp.where(lon_even, first[...], last[...])
    ca_ref[...] = a.astype(BF16)
    cb_ref[...] = b.astype(BF16)


def gelu(x):
    inner = np.float32(np.sqrt(2 / np.pi)) * (x + np.float32(0.044715) * (x * x * x))
    return x * (np.float32(0.5) * (np.float32(1.0) + jnp.tanh(inner)))


def mix_kernel(
    flags, e_ref, ra_ref, rb_ref, ca_ref, cb_ref, land_ref, taps_ref, w_hbm, stream_ref, perm_ref,
    mixed_ref, out_ref, w_buf, act, total, sem, *, chunk,
):
    rows, cols, width_exp = e_ref.shape
    tokens = rows * cols
    steps = width_exp // chunk

    def fetch(i):
        return pltpu.make_async_copy(
            w_hbm.at[pl.ds(i * chunk, chunk), :], w_buf.at[pl.ds(i * chunk, chunk), :], sem.at[i]
        )

    for i in range(steps):
        fetch(i).start()
    lat_even = flags[0] == 1
    lon_even = flags[1] == 1
    sub = lax.broadcasted_iota(jnp.int32, (cols, 128), 0)
    is_first = sub == 0
    is_last = sub == cols - 1

    def depthwise(at):
        lanes = pl.ds(at, 128)
        ra = ra_ref[:, lanes].astype(F32)
        rb = rb_ref[:, lanes].astype(F32)
        x = [jnp.where(lat_even, rb, ra)]
        x += [e_ref[r, :, lanes].astype(F32) for r in range(rows)]
        x += [jnp.where(lat_even, ra, rb)]
        ca = ca_ref[:, lanes].astype(F32)
        cb = cb_ref[:, lanes].astype(F32)
        left = jnp.where(lon_even, cb, ca)
        right = jnp.where(lon_even, ca, cb)
        tap = [[taps_ref[3 * a + b : 3 * a + b + 1, lanes] for b in range(3)] for a in range(3)]
        shift = taps_ref[9:10, lanes]
        from_left = sum(tap[a][0] * left[a : a + rows] for a in range(3))
        from_right = sum(tap[a][2] * right[a : a + rows] for a in range(3))
        for r in range(rows):
            y = [tap[0][b] * x[r] + tap[1][b] * x[r + 1] + tap[2][b] * x[r + 2] for b in range(3)]
            y0 = jnp.where(is_first, from_left[r : r + 1], pltpu.roll(y[0], 1, 0))
            y2 = jnp.where(is_last, from_right[r : r + 1], pltpu.roll(y[2], cols - 1, 0))
            filtered = land_ref[r] * shift + y[1] + (y0 + y2)
            act[r * cols : (r + 1) * cols, lanes] = gelu(filtered).astype(BF16)

    def conv(i):
        for k in range(chunk // 128):
            depthwise(pl.multiple_of(i * chunk + k * 128, 128))

    def project(i):
        at = pl.multiple_of(i * chunk, chunk)
        return jnp.dot(
            act[:, pl.ds(at, chunk)], w_buf[pl.ds(at, chunk), :], preferred_element_type=F32
        )

    total[...] = stream_ref[...].astype(F32)
    conv(0)

    def step(i, carry):
        fetch(i - 1).wait()
        conv(i)
        total[...] += project(i - 1)
        return carry

    lax.fori_loop(1, steps, step, 0)
    fetch(steps - 1).wait()
    mixed = (total[...] + project(steps - 1)).astype(BF16)
    mixed_ref[...] = mixed
    flat = mixed.astype(F32)
    centred = flat - jnp.mean(flat, axis=1, keepdims=True)
    spread = jnp.mean(centred * centred, axis=1, keepdims=True)
    normed = (centred * lax.rsqrt(spread + EPS)).astype(BF16)
    sent = jnp.dot(perm_ref[...], normed, preferred_element_type=F32)
    for k in range(tokens // 4):
        out_ref[k] = sent[4 * k : 4 * k + 4].astype(BF16)


def attend_kernel(x_ref, w_ref, bias_ref, out_ref, x_buf, o_buf, *, heads):
    tokens = 4 * x_ref.shape[0]
    width = x_ref.shape[2]
    head_dim = width // heads
    for k in range(tokens // 4):
        x_buf[4 * k : 4 * k + 4, :] = x_ref[k].astype(F32)
    x = x_buf[...].astype(BF16)
    scale = np.float32(head_dim**-0.5)
    per = 128 // head_dim
    lane_head = lax.broadcasted_iota(jnp.int32, (tokens, 128), 1) // head_dim
    ones = jnp.ones((16, tokens), BF16)

    def project(col):
        return jnp.dot(x, w_ref[:, col : col + 128], preferred_element_type=F32)

    for p in range(heads // per):
        q = project(128 * p)
        k = project(width + 128 * p).astype(BF16)
        v = project(2 * width + 128 * p)
        v_t = jnp.concatenate([jnp.transpose(v).astype(BF16), ones], axis=0)
        queries = jnp.concatenate(
            [jnp.where(lane_head == j, q, 0.0).astype(BF16) for j in range(per)], axis=0
        )
        scores = lax.dot_general(
            k, queries, (((1,), (1,)), ((), ())), preferred_element_type=F32
        )
        weights = []
        for j in range(per):
            base = bias_ref[p * per + j]
            bias = jnp.concatenate(
                [base if n == 0 else pltpu.roll(base, 16 * n, 1) for n in range(GRID)], axis=0
            )
            s = scores[:, tokens * j : tokens * (j + 1)] * scale + bias
            weights.append(jnp.exp(s - jnp.max(s, axis=0, keepdims=True)).astype(BF16))
        summed = jnp.dot(v_t, jnp.concatenate(weights, axis=1), preferred_element_type=F32)
        parts = []
        for j in range(per):
            block = summed[:, tokens * j : tokens * (j + 1)]
            parts.append(
                block[head_dim * j : head_dim * (j + 1)] * (1.0 / block[128 : 129])
            )
        o_buf[:, 128 * p : 128 * (p + 1)] = jnp.transpose(jnp.concatenate(parts, axis=0))
    for k in range(tokens // 4):
        out_ref[k] = o_buf[4 * k : 4 * k + 4, :].astype(BF16)


def out_kernel(a_ref, w_ref, mixed_ref, perm_ref, out_ref, a_buf):
    tokens = 4 * a_ref.shape[0]
    for k in range(tokens // 4):
        a_buf[4 * k : 4 * k + 4, :] = a_ref[k].astype(F32)
    attended = jnp.dot(
        perm_ref[...], a_buf[...].astype(BF16), preferred_element_type=F32
    ).astype(BF16)
    result = mixed_ref[...].astype(F32) + jnp.dot(
        attended, w_ref[...], preferred_element_type=F32
    )
    out_ref[...] = result.astype(BF16)


def bias_choice():
    side = 2 * GRID - 1
    choose = np.zeros((side * GRID, 2 * GRID, 128), np.float32)
    block = np.full((2 * GRID, 128), NEG, np.float32)
    for mk in range(GRID):
        for gk in range(2):
            for nq in range(GRID):
                for mq in range(GRID):
                    for gq in range(2):
                        r, q = 2 * mk + gk, 16 * nq + 2 * mq + gq
                        choose[(mk - mq + GRID - 1) * GRID + (-nq) % GRID, r, q] = 1.0
                        if gk == gq:
                            block[r, q] = 0.0
    return choose, block


def local(expanded, stream, land, polar, land_shift, dw_kernel, w_proj, w_qkv, w_out, rel_bias):
    rows, cols, width_exp = expanded.shape
    width = stream.shape[2]
    heads = rel_bias.shape[0]
    tokens = rows * cols
    lon, lat = ("nhi", "nlo"), "lat"
    lons, lats = lax.axis_size(lon), lax.axis_size(lat)
    everyone = lon + (lat,)
    lat_at = lax.axis_index(lat)
    lon_at = lax.axis_index(lon)
    lat_even = lat_at % 2 == 0
    lon_even = lon_at % 2 == 0
    flags = jnp.stack([lat_even, lon_even]).astype(jnp.int32)
    top_row, bottom_row = expanded[0], expanded[rows - 1]
    row_a = jnp.where(lat_even, bottom_row, top_row)
    row_b = jnp.where(lat_even, top_row, bottom_row)
    got_a = lax.ppermute(row_a, lat, [(i, i ^ 1) for i in range(lats)])
    got_b = lax.ppermute(
        row_b, lat, [(i, j) for k in range(1, lats - 1, 2) for i, j in ((k, k + 1), (k + 1, k))]
    )
    col_shape = jax.ShapeDtypeStruct((rows + 2, width_exp), BF16)
    col_a, col_b = pl.pallas_call(
        pack_columns,
        name="pack_columns",
        out_shape=(col_shape, col_shape),
        in_specs=[SM, VM, VM, VM],
        out_specs=(VM, VM),
        scratch_shapes=[pltpu.VMEM((rows + 2, width_exp), F32)] * 2,
    )(flags, expanded, got_a, got_b)
    seen_b = lax.ppermute(
        col_b, lon, [(i, (i + 1) % lons if i % 2 else (i - 1) % lons) for i in range(lons)]
    )
    seen_a = lax.ppermute(col_a, lon, [(i, i ^ 1) for i in range(lons)])

    order = send_order(rows, cols)
    perm = np.zeros((tokens, tokens), np.float32)
    perm[np.arange(tokens), order] = 1.0
    perm_send = jnp.asarray(perm, BF16)
    perm_back = jnp.asarray(perm.T, BF16)
    taps = jnp.concatenate([dw_kernel.reshape(9, width_exp), land_shift[None]], axis=0)
    land_lanes = jnp.broadcast_to(land.astype(F32)[:, :, None], (rows, cols, 128))
    chunk = 256
    steps = width_exp // chunk
    mixed, sent = pl.pallas_call(
        functools.partial(mix_kernel, chunk=chunk),
        name="mix",
        out_shape=(
            jax.ShapeDtypeStruct((tokens, width), BF16),
            jax.ShapeDtypeStruct((tokens // 4, 4, width), BF16),
        ),
        in_specs=[SM] + [VM] * 7 + [HBM] + [VM] * 2,
        out_specs=(VM, VM),
        scratch_shapes=[
            pltpu.VMEM((width_exp, width), BF16),
            pltpu.VMEM((tokens, width_exp), BF16),
            pltpu.VMEM((tokens, width), F32),
            pltpu.SemaphoreType.DMA((steps,)),
        ],
        compiler_params=pltpu.CompilerParams(vmem_limit_bytes=24 << 20),
    )(
        flags, expanded, got_a, got_b, seen_a, seen_b, land_lanes, taps, w_proj,
        stream.reshape(tokens, width), perm_send,
    )
    choose, block = bias_choice()
    strips = rows // 2
    strip = lax.axis_index("nhi") * strips // lax.axis_size("nhi")
    capped = lax.dynamic_index_in_dim(polar.reshape(GRID, strips), strip, 1, keepdims=False)
    bias = jnp.einsum(
        "hs,srq->hrq", rel_bias.reshape(heads, -1), choose, precision=lax.Precision.HIGHEST
    )
    hidden = jnp.where(jnp.repeat(capped, 2)[:, None] == 1, np.float32(NEG), block)
    bias = bias + hidden[None]

    group = ("nhi", lat)
    mine = lax.all_to_all(sent, group, 0, 0, tiled=True)
    attended = pl.pallas_call(
        functools.partial(attend_kernel, heads=heads),
        name="attend",
        out_shape=jax.ShapeDtypeStruct((tokens // 4, 4, width), BF16),
        in_specs=[VM] * 3,
        out_specs=VM,
        scratch_shapes=[pltpu.VMEM((tokens, width), F32)] * 2,
        compiler_params=pltpu.CompilerParams(vmem_limit_bytes=24 << 20),
    )(mine, w_qkv, bias)
    back = lax.all_to_all(attended, group, 0, 0, tiled=True)
    result = pl.pallas_call(
        out_kernel,
        name="out",
        out_shape=jax.ShapeDtypeStruct((tokens, width), BF16),
        in_specs=[VM] * 4,
        out_specs=VM,
        scratch_shapes=[pltpu.VMEM((tokens, width), F32)],
    )(back, w_out, mixed, perm_back)
    return result.reshape(rows, cols, width)


def solution(mesh):
    lons, lats = mesh.shape["lon"], mesh.shape["lat"]
    fine = Mesh(mesh.devices.reshape(GRID, lons // GRID, lats), ("nhi", "nlo", "lat"))
    lon = ("nhi", "nlo")
    in_specs = (P("lat", lon, None), P("lat", lon, None), P("lat", lon)) + (P(),) * 7
    return jax.shard_map(
        local, mesh=fine, in_specs=in_specs, out_specs=P("lat", lon, None), check_vma=False
    )
```

```python
import functools

import jax
import jax.numpy as jnp
import numpy as np
from jax import lax
from jax.experimental import pallas as pl
from jax.experimental.pallas import tpu as pltpu
from jax.sharding import Mesh
from jax.sharding import PartitionSpec as P

GRID = 8
EPS = 1e-05
NEG = -1e30
F32 = jnp.float32
BF16 = jnp.bfloat16
VM = pl.BlockSpec(memory_space=pltpu.VMEM)
SM = pl.BlockSpec(memory_space=pltpu.SMEM)
HBM = pl.BlockSpec(memory_space=pltpu.HBM)


def in_hbm(x):
    return pltpu.with_memory_space_constraint(x, pltpu.HBM)


def send_matrix(rows, cols, back):
    tokens = rows * cols
    strips, pairs = rows // 2, cols // 2
    to = lax.broadcasted_iota(jnp.int32, (tokens, tokens), 0)
    at = lax.broadcasted_iota(jnp.int32, (tokens, tokens), 1)
    if back:
        to, at = at, to
    s, rest = to // (4 * pairs), to % (4 * pairs)
    c2, m, c1 = rest // 4, rest % 4 // 2, rest % 2
    token = (m * strips + s) * cols + 2 * c2 + c1
    return jnp.where(token == at, 1.0, 0.0).astype(BF16)


def even(axes):
    return lax.rem(lax.axis_index(axes), 2) == 0


def stage_kernel(e_hbm, row_ref, e_ref, ca_ref, cb_ref, first, last, sem, *, lon):
    rows, cols, _ = e_ref.shape
    copies = [
        pltpu.make_async_copy(e_hbm.at[r], e_ref.at[r], sem.at[r]) for r in range(rows)
    ]
    for copy in copies:
        copy.start()
    for r in range(rows):
        copies[r].wait()
        line = e_ref[r].astype(F32)
        first[r : r + 1, :] = line[0:1]
        last[r : r + 1, :] = line[cols - 1 : cols]
    lon_even = even(lon)
    ca_ref[...] = jnp.where(lon_even, last[...], first[...]).astype(BF16)
    cb_ref[...] = jnp.where(lon_even, first[...], last[...]).astype(BF16)


def pack_kernel(ca_ref, cb_ref, ra_ref, rb_ref, oa_ref, ob_ref, *, lat, lon):
    lat_even, lon_even = even(lat), even(lon)
    cols = ra_ref.shape[0]
    ra = ra_ref[...].astype(F32)
    rb = rb_ref[...].astype(F32)
    top = jnp.where(lat_even, rb, ra)
    bottom = jnp.where(lat_even, ra, rb)
    for c_ref, o_ref, is_last in ((ca_ref, oa_ref, lon_even), (cb_ref, ob_ref, ~lon_even)):
        above = jnp.where(is_last, top[cols - 1 : cols], top[0:1])
        below = jnp.where(is_last, bottom[cols - 1 : cols], bottom[0:1])
        o_ref[...] = jnp.concatenate([above, c_ref[...].astype(F32), below], axis=0).astype(BF16)


def gelu(x):
    inner = x * (np.float32(np.sqrt(2 / np.pi)) + np.float32(0.044715 * np.sqrt(2 / np.pi)) * (x * x))
    half = np.float32(0.5) * x
    return half + half * jnp.tanh(inner)


def normalize(flat):
    centred = flat - jnp.mean(flat, axis=1, keepdims=True)
    spread = jnp.mean(centred * centred, axis=1, keepdims=True)
    return centred * lax.rsqrt(spread + EPS)


def fill_bias(polar, rel, out_ref, strips, nhi):
    strip = lax.axis_index(nhi) * strips // lax.axis_size(nhi)
    high = rel.astype(BF16)
    middle = (rel - high.astype(F32)).astype(BF16)
    low = (rel - high.astype(F32) - middle.astype(F32)).astype(BF16)
    offsets = rel.shape[0]
    lane = lax.broadcasted_iota(jnp.int32, (offsets, 128), 1)
    mq = lane // 2 % GRID
    nq = lane // (2 * GRID)
    at = lax.broadcasted_iota(jnp.int32, (offsets, 128), 0)
    gq = lax.broadcasted_iota(jnp.int32, (1, 128), 1) % 2
    for mk in range(GRID):
        wanted = (mk - mq + GRID - 1) * GRID + (GRID - nq) % GRID
        choose = jnp.where(at == wanted, 1.0, 0.0).astype(BF16)
        near = sum(
            lax.dot_general(
                part, choose, (((0,), (0,)), ((), ())), preferred_element_type=F32
            )
            for part in (high, middle, low)
        )
        cap = jnp.where(polar[mk * strips + strip] == 1, np.float32(NEG), np.float32(0.0))
        for gk in range(2):
            out_ref[:, 2 * mk + gk, :] = near + jnp.where(gq == gk, cap, np.float32(NEG))


def mix_kernel(
    e_ref, ra_ref, rb_ref, land_hbm, taps_hbm, shift_hbm, w_hbm, stream_hbm, qkv_hbm, out_hbm,
    rel_hbm, polar_hbm,
    mixed_ref, sent_ref, edge_ref, taps_ref, w_ref, stream_ref, qkv_ref, wout_ref, bias_ref,
    rel_ref, polar_ref, land_ref, shift_ref, act, total, land_lanes, perm_ref, sem, *, chunk, lat,
):
    rows, cols, width_exp = e_ref.shape
    tokens = rows * cols
    steps = width_exp // chunk

    def fetch(i):
        part = pl.ds(i * chunk, chunk)
        return pltpu.make_async_copy(w_hbm.at[part], w_ref.at[part], sem.at[i])

    first = [
        pltpu.make_async_copy(src, dst, sem.at[steps + i])
        for i, (src, dst) in enumerate(
            ((land_hbm, land_ref), (taps_hbm, taps_ref), (shift_hbm, shift_ref))
        )
    ]
    later = [
        pltpu.make_async_copy(src, dst, sem.at[steps + 3 + i])
        for i, (src, dst) in enumerate(
            (
                (stream_hbm, stream_ref), (rel_hbm, rel_ref), (polar_hbm, polar_ref),
                (qkv_hbm, qkv_ref), (out_hbm, wout_ref),
            )
        )
    ]
    for copy in first:
        copy.start()
    for i in range(steps):
        fetch(i).start()
    for copy in later:
        copy.start()
    lat_even = even(lat)
    perm_ref[...] = send_matrix(rows, cols, False)
    sub = lax.broadcasted_iota(jnp.int32, (cols, 128), 0)
    is_first = sub == 0
    is_last = sub == cols - 1
    token = lax.broadcasted_iota(jnp.int32, (tokens, cols), 0)
    at = lax.broadcasted_iota(jnp.int32, (tokens, cols), 1)
    row_of = lax.broadcasted_iota(jnp.int32, (tokens, rows), 0) // cols
    pick_row = (row_of == lax.broadcasted_iota(jnp.int32, (tokens, rows), 1)).astype(F32)
    for copy in first:
        copy.wait()
    by_row = jnp.dot(pick_row, land_ref[...].astype(F32), preferred_element_type=F32)
    mine = jnp.where(lax.rem(token, cols) == at, by_row, 0.0)
    land_lanes[...] = jnp.dot(mine, jnp.ones((cols, 128), F32), preferred_element_type=F32)

    def depthwise(at):
        lanes = pl.ds(at, 128)
        ra = ra_ref[:, lanes].astype(F32)
        rb = rb_ref[:, lanes].astype(F32)
        x = [jnp.where(lat_even, rb, ra)]
        x += [e_ref[r, :, lanes].astype(F32) for r in range(rows)]
        x += [jnp.where(lat_even, ra, rb)]
        tap = [[taps_ref[a, b : b + 1, lanes] for b in range(3)] for a in range(3)]
        shift = shift_ref[:, lanes]
        for r in range(rows):
            y = [tap[0][b] * x[r] + tap[1][b] * x[r + 1] + tap[2][b] * x[r + 2] for b in range(3)]
            y0 = jnp.where(is_first, 0.0, pltpu.roll(y[0], 1, 0))
            y2 = jnp.where(is_last, 0.0, pltpu.roll(y[2], cols - 1, 0))
            filtered = land_lanes[r * cols : (r + 1) * cols] * shift + y[1] + (y0 + y2)
            edge_ref[r : r + 1, lanes] = filtered[0:1]
            edge_ref[rows + r : rows + r + 1, lanes] = filtered[cols - 1 : cols]
            act[r * cols : (r + 1) * cols, lanes] = gelu(filtered).astype(BF16)

    def conv(i):
        for k in range(chunk // 128):
            depthwise(pl.multiple_of(i * chunk + k * 128, 128))

    def project(i):
        at = pl.multiple_of(i * chunk, chunk)
        return jnp.dot(
            act[:, pl.ds(at, chunk)], w_ref[pl.ds(at, chunk), :], preferred_element_type=F32
        )

    total[...] = jnp.zeros_like(total)
    conv(0)

    def step(i, carry):
        fetch(i - 1).wait()
        conv(i)
        total[...] += project(i - 1)
        return carry

    lax.fori_loop(1, steps, step, 0)
    fetch(steps - 1).wait()
    later[0].wait()
    stream = stream_ref[...].reshape(tokens, stream_ref.shape[2]).astype(F32)
    mixed = (stream + (total[...] + project(steps - 1))).astype(BF16)
    mixed_ref[...] = mixed
    normed = normalize(mixed.astype(F32)).astype(BF16)
    sent = jnp.dot(perm_ref[...], normed, preferred_element_type=F32)
    for k in range(tokens // 4):
        sent_ref[k] = sent[4 * k : 4 * k + 4].astype(BF16)
    for copy in later[1:]:
        copy.wait()
    fill_bias(polar_ref, rel_ref[...], bias_ref, rows // 2, "nhi")


def edge_kernel(
    edge_ref, ca_ref, cb_ref, taps_ref, w_ref, stream_ref, sent_ref, inner_ref, mixed_ref, out_ref, act,
    *, lon, chunk,
):
    double, width_exp = edge_ref.shape
    rows = double // 2
    lon_even = even(lon)
    for i in range(width_exp // chunk):
        lanes = slice(i * chunk, (i + 1) * chunk)
        ca = ca_ref[:, lanes].astype(F32)
        cb = cb_ref[:, lanes].astype(F32)
        left = jnp.where(lon_even, cb, ca)
        right = jnp.where(lon_even, ca, cb)
        from_left = sum(taps_ref[a, 0:1, lanes] * left[a : a + rows] for a in range(3))
        from_right = sum(taps_ref[a, 2:3, lanes] * right[a : a + rows] for a in range(3))
        filtered = edge_ref[:, lanes] + jnp.concatenate([from_left, from_right], axis=0)
        act[:, lanes] = gelu(filtered).astype(BF16)
    projected = jnp.dot(act[...], w_ref[...], preferred_element_type=F32)
    cols = stream_ref.shape[1]
    first = jnp.concatenate([stream_ref[r, 0:1].astype(F32) for r in range(rows)], axis=0)
    last = jnp.concatenate([stream_ref[r, cols - 1 : cols].astype(F32) for r in range(rows)], axis=0)
    mixed = (jnp.concatenate([first, last], axis=0) + projected).astype(BF16)
    mixed = mixed.astype(F32)
    normed = normalize(mixed).astype(BF16).astype(F32)
    sub = lax.broadcasted_iota(jnp.int32, (cols, mixed.shape[1]), 0)
    for r in range(rows):
        part = slice(r * cols, (r + 1) * cols)
        inner = inner_ref[part].astype(F32)
        inner = jnp.where(sub == 0, mixed[r : r + 1], inner)
        inner = jnp.where(sub == cols - 1, mixed[rows + r : rows + r + 1], inner)
        mixed_ref[part] = inner.astype(BF16)
    out_ref[...] = sent_ref[...]
    pairs = cols // 2
    strips = rows // 2
    for s in range(strips):
        for side, c2 in ((0, 0), (1, pairs - 1)):
            k = s * pairs + c2
            old = sent_ref[k].astype(F32)
            keep = [old[0:1], old[1:2], old[2:3], old[3:4]]
            for m in range(2):
                at = side * rows + m * strips + s
                keep[2 * m + side] = normed[at : at + 1]
            out_ref[k] = jnp.concatenate(keep, axis=0).astype(BF16)


def attend_kernel(x_ref, w_ref, bias_ref, out_ref, x_buf, o_buf, *, heads):
    tokens = 4 * x_ref.shape[0]
    width = x_ref.shape[2]
    head_dim = width // heads
    for k in range(tokens // 4):
        x_buf[4 * k : 4 * k + 4, :] = x_ref[k].astype(F32)
    x = x_buf[...].astype(BF16)
    scale = np.float32(head_dim**-0.5)
    per = 128 // head_dim
    lane_head = lax.broadcasted_iota(jnp.int32, (tokens, 128), 1) // head_dim
    ones = jnp.ones((16, tokens), BF16)

    def project(col):
        return jnp.dot(x, w_ref[:, col : col + 128], preferred_element_type=F32)

    for p in range(heads // per):
        q = project(128 * p)
        k = project(width + 128 * p).astype(BF16)
        v = project(2 * width + 128 * p)
        v_t = jnp.concatenate([jnp.transpose(v).astype(BF16), ones], axis=0)
        queries = jnp.concatenate(
            [jnp.where(lane_head == j, q, 0.0).astype(BF16) for j in range(per)], axis=0
        )
        scores = lax.dot_general(
            k, queries, (((1,), (1,)), ((), ())), preferred_element_type=F32
        )
        weights = []
        for j in range(per):
            base = bias_ref[p * per + j]
            bias = jnp.concatenate(
                [base if n == 0 else pltpu.roll(base, 16 * n, 1) for n in range(GRID)], axis=0
            )
            s = scores[:, tokens * j : tokens * (j + 1)] * scale + bias
            weights.append(jnp.exp(s - jnp.max(s, axis=0, keepdims=True)).astype(BF16))
        summed = jnp.dot(v_t, jnp.concatenate(weights, axis=1), preferred_element_type=F32)
        parts = []
        for j in range(per):
            block = summed[:, tokens * j : tokens * (j + 1)]
            parts.append(
                block[head_dim * j : head_dim * (j + 1)] * (1.0 / block[128 : 129])
            )
        o_buf[:, 128 * p : 128 * (p + 1)] = jnp.transpose(jnp.concatenate(parts, axis=0))
    for k in range(tokens // 4):
        out_ref[k] = o_buf[4 * k : 4 * k + 4, :].astype(BF16)


def out_kernel(a_ref, w_ref, mixed_ref, out_ref, a_buf, *, rows, cols):
    tokens = rows * cols
    for k in range(tokens // 4):
        a_buf[4 * k : 4 * k + 4, :] = a_ref[k].astype(F32)
    attended = jnp.dot(
        send_matrix(rows, cols, True), a_buf[...].astype(BF16), preferred_element_type=F32
    ).astype(BF16)
    result = mixed_ref[...].astype(F32) + jnp.dot(
        attended, w_ref[...], preferred_element_type=F32
    )
    out_ref[...] = result.astype(BF16)


def local(expanded, stream, land, polar, land_shift, dw_kernel, w_proj, w_qkv, w_out, rel_bias):
    rows, cols, width_exp = expanded.shape
    width = stream.shape[2]
    heads = rel_bias.shape[0]
    tokens = rows * cols
    lon, lat = ("nhi", "nlo"), "lat"
    lons, lats = lax.axis_size(lon), lax.axis_size(lat)
    everyone = lon + (lat,)
    lat_even = lax.axis_index(lat) % 2 == 0
    top_row, bottom_row = expanded[0], expanded[rows - 1]
    row_a = jnp.where(lat_even, bottom_row, top_row)
    row_b = jnp.where(lat_even, top_row, bottom_row)
    got_a = lax.ppermute(row_a, lat, [(i, i ^ 1) for i in range(lats)])
    got_b = lax.ppermute(
        row_b, lat, [(i, j) for k in range(1, lats - 1, 2) for i, j in ((k, k + 1), (k + 1, k))]
    )
    col_shape = jax.ShapeDtypeStruct((rows, width_exp), BF16)
    e_here, own_a, own_b = pl.pallas_call(
        functools.partial(stage_kernel, lon=lon),
        name="stage",
        out_shape=(pltpu.VMEM(expanded.shape, BF16), col_shape, col_shape),
        in_specs=[HBM, VM],
        out_specs=(VM, VM, VM),
        scratch_shapes=[pltpu.VMEM((rows, width_exp), F32)] * 2 + [pltpu.SemaphoreType.DMA((rows,))],
        compiler_params=pltpu.CompilerParams(vmem_limit_bytes=4 << 20),
        cost_estimate=pl.CostEstimate(flops=10**6, bytes_accessed=2 * 10**6, transcendentals=0),
    )(in_hbm(expanded), row_b)
    col_shape = jax.ShapeDtypeStruct((rows + 2, width_exp), BF16)
    col_a, col_b = pl.pallas_call(
        functools.partial(pack_kernel, lat=lat, lon=lon),
        name="pack",
        out_shape=(col_shape, col_shape),
        in_specs=[VM] * 4,
        out_specs=(VM, VM),
        compiler_params=pltpu.CompilerParams(vmem_limit_bytes=4 << 20),
    )(own_a, own_b, got_a, got_b)
    seen_b = lax.ppermute(
        col_b, lon, [(i, (i + 1) % lons if i % 2 else (i - 1) % lons) for i in range(lons)]
    )
    seen_a = lax.ppermute(col_a, lon, [(i, i ^ 1) for i in range(lons)])

    chunk = 256
    token_shape = jax.ShapeDtypeStruct((tokens, width), BF16)
    sent_shape = jax.ShapeDtypeStruct((tokens // 4, 4, width), BF16)
    steps = width_exp // chunk
    rel = jnp.transpose(rel_bias, (1, 2, 0)).reshape(-1, heads)
    mixed, sent, edge, taps, w_proj, stream, w_qkv, w_out, bias = pl.pallas_call(
        functools.partial(mix_kernel, chunk=chunk, lat=lat),
        name="mix",
        out_shape=(
            token_shape, sent_shape, pltpu.VMEM((2 * rows, width_exp), F32),
            pltpu.VMEM(dw_kernel.shape, F32),
            pltpu.VMEM(w_proj.shape, BF16),
            pltpu.VMEM(stream.shape, BF16),
            pltpu.VMEM(w_qkv.shape, BF16),
            pltpu.VMEM(w_out.shape, BF16),
            pltpu.VMEM((heads, 2 * GRID, 128), F32),
        ),
        in_specs=[VM] * 3 + [HBM] * 9,
        out_specs=(VM,) * 9,
        scratch_shapes=[
            pltpu.VMEM(rel.shape, F32),
            pltpu.SMEM(polar.shape, jnp.int32),
            pltpu.VMEM((rows, cols), jnp.int32),
            pltpu.VMEM((1, width_exp), F32),
            pltpu.VMEM((tokens, width_exp), BF16),
            pltpu.VMEM((tokens, width), F32),
            pltpu.VMEM((tokens, 128), F32),
            pltpu.VMEM((tokens, tokens), BF16),
            pltpu.SemaphoreType.DMA((steps + 8,)),
        ],
        compiler_params=pltpu.CompilerParams(vmem_limit_bytes=20 << 20),
        cost_estimate=pl.CostEstimate(flops=10**9, bytes_accessed=10**6, transcendentals=0),
    )(
        e_here, got_a, got_b,
        *map(in_hbm, (land, dw_kernel, land_shift[None], w_proj, stream, w_qkv, w_out, rel, polar)),
    )
    mixed, sent = pl.pallas_call(
        functools.partial(edge_kernel, lon=lon, chunk=chunk),
        name="edge",
        out_shape=(token_shape, sent_shape),
        in_specs=[VM] * 8,
        out_specs=(VM, VM),
        scratch_shapes=[pltpu.VMEM((2 * rows, width_exp), BF16)],
        compiler_params=pltpu.CompilerParams(vmem_limit_bytes=8 << 20),
    )(edge, seen_a, seen_b, taps, w_proj, stream, sent, mixed)
    group = ("nhi", lat)
    mine = lax.all_to_all(sent, group, 0, 0, tiled=True)
    attended = pl.pallas_call(
        functools.partial(attend_kernel, heads=heads),
        name="attend",
        out_shape=jax.ShapeDtypeStruct((tokens // 4, 4, width), BF16),
        in_specs=[VM] * 3,
        out_specs=VM,
        scratch_shapes=[pltpu.VMEM((tokens, width), F32)] * 2,
        compiler_params=pltpu.CompilerParams(vmem_limit_bytes=8 << 20),
    )(mine, w_qkv, bias)
    back = lax.all_to_all(attended, group, 0, 0, tiled=True)
    result = pl.pallas_call(
        functools.partial(out_kernel, rows=rows, cols=cols),
        name="out",
        out_shape=jax.ShapeDtypeStruct((tokens, width), BF16),
        in_specs=[VM] * 3,
        out_specs=VM,
        scratch_shapes=[pltpu.VMEM((tokens, width), F32)],
        compiler_params=pltpu.CompilerParams(vmem_limit_bytes=8 << 20),
    )(back, w_out, mixed)
    return result.reshape(rows, cols, width)


def solution(mesh):
    lons, lats = mesh.shape["lon"], mesh.shape["lat"]
    fine = Mesh(mesh.devices.reshape(GRID, lons // GRID, lats), ("nhi", "nlo", "lat"))
    lon = ("nhi", "nlo")
    in_specs = (P("lat", lon, None), P("lat", lon, None), P("lat", lon)) + (P(),) * 7
    return jax.shard_map(
        local, mesh=fine, in_specs=in_specs, out_specs=P("lat", lon, None), check_vma=False
    )
```

```python
import functools

import jax
import jax.numpy as jnp
import numpy as np
from jax import lax
from jax.experimental import pallas as pl
from jax.experimental.pallas import tpu as pltpu
from jax.sharding import Mesh
from jax.sharding import PartitionSpec as P

GRID = 8
EPS = 1e-05
NEG = -1e30
LOG2E = np.float32(np.log2(np.e))
F32 = jnp.float32
BF16 = jnp.bfloat16
VM = pl.BlockSpec(memory_space=pltpu.VMEM)
SM = pl.BlockSpec(memory_space=pltpu.SMEM)
HBM = pl.BlockSpec(memory_space=pltpu.HBM)


def in_hbm(x):
    return pltpu.with_memory_space_constraint(x, pltpu.HBM)


def send_matrix(rows, cols, back):
    tokens = rows * cols
    strips, pairs = rows // 2, cols // 2
    to = lax.broadcasted_iota(jnp.int32, (tokens, tokens), 0)
    at = lax.broadcasted_iota(jnp.int32, (tokens, tokens), 1)
    if back:
        to, at = at, to
    s, rest = to // (4 * pairs), to % (4 * pairs)
    c2, m, c1 = rest // 4, rest % 4 // 2, rest % 2
    token = (m * strips + s) * cols + 2 * c2 + c1
    return jnp.where(token == at, 1.0, 0.0).astype(BF16)


def even(axes):
    return lax.rem(lax.axis_index(axes), 2) == 0


def pick_kernel(*refs, lat, lon):
    ins, outs, refs = refs[:5], refs[5:10], refs[10:]
    xa_ref, xb_ref, ra_ref, rb_ref, ca_ref, cb_ref, first, last, sem = refs
    e_hbm, e_ref = ins[0], outs[0]
    rows, cols, _ = e_ref.shape
    lines = [pltpu.make_async_copy(e_hbm.at[r], e_ref.at[r], sem.at[r]) for r in range(rows)]
    rest = [
        pltpu.make_async_copy(src, dst, sem.at[rows + i])
        for i, (src, dst) in enumerate(zip(ins[1:], outs[1:]))
    ]
    for copy in lines + rest:
        copy.start()
    for r in range(rows):
        lines[r].wait()
        line = e_ref[r].astype(F32)
        first[r : r + 1, :] = line[0:1]
        last[r : r + 1, :] = line[cols - 1 : cols]
    lat_even, lon_even = even(lat), even(lon)
    top = e_ref[0].astype(F32)
    bottom = e_ref[rows - 1].astype(F32)
    ra_ref[...] = jnp.where(lat_even, bottom, top).astype(BF16)
    rb_ref[...] = jnp.where(lat_even, top, bottom).astype(BF16)
    a, b = first[...], last[...]
    ca_ref[...] = jnp.where(lon_even, b, a).astype(BF16)
    cb_ref[...] = jnp.where(lon_even, a, b).astype(BF16)
    above = jnp.concatenate([a[0:1], b[0:1]], axis=0)
    below = jnp.concatenate([a[rows - 1 : rows], b[rows - 1 : rows]], axis=0)
    xa_ref[...] = jnp.where(lat_even, below, above).astype(BF16)
    xb_ref[...] = jnp.where(lat_even, above, below).astype(BF16)
    for copy in rest:
        copy.wait()


def pack_kernel(ca_ref, cb_ref, xa_ref, xb_ref, oa_ref, ob_ref, *, lat, lon):
    lat_even, lon_even = even(lat), even(lon)
    rows, width_exp = ca_ref.shape
    half = rows // 2
    part = width_exp // half
    xa, xb = xa_ref[...].astype(F32), xb_ref[...].astype(F32)
    ends = jnp.where(lat_even, xb, xa), jnp.where(lat_even, xa, xb)
    for c_ref, o_ref, is_last in ((ca_ref, oa_ref, lon_even), (cb_ref, ob_ref, ~lon_even)):
        o_ref[:, :width_exp] = c_ref[...]
        cells = [jnp.where(is_last, end[1:2], end[0:1]) for end in ends]
        quarters = [cell[:, part * k : part * (k + 1)] for cell in cells for k in range(half)]
        o_ref[:, width_exp:] = jnp.concatenate(quarters, axis=0).astype(BF16)


def gelu(x):
    inner = x * (np.float32(np.sqrt(2 / np.pi)) + np.float32(0.044715 * np.sqrt(2 / np.pi)) * (x * x))
    half = np.float32(0.5) * x
    return half + half * jnp.tanh(inner)


def normalize(flat):
    centred = flat - jnp.mean(flat, axis=1, keepdims=True)
    spread = jnp.mean(centred * centred, axis=1, keepdims=True)
    return centred * lax.rsqrt(spread + EPS)


def fill_bias(polar, rel, out_ref, strips, nhi):
    strip = lax.axis_index(nhi) * strips // lax.axis_size(nhi)
    high = rel.astype(BF16)
    middle = (rel - high.astype(F32)).astype(BF16)
    low = (rel - high.astype(F32) - middle.astype(F32)).astype(BF16)
    offsets = rel.shape[0]
    lane = lax.broadcasted_iota(jnp.int32, (offsets, 128), 1)
    mq = lane // 2 % GRID
    nq = lane // (2 * GRID)
    at = lax.broadcasted_iota(jnp.int32, (offsets, 128), 0)
    gq = lax.broadcasted_iota(jnp.int32, (1, 128), 1) % 2
    for mk in range(GRID):
        wanted = (mk - mq + GRID - 1) * GRID + (GRID - nq) % GRID
        choose = jnp.where(at == wanted, 1.0, 0.0).astype(BF16)
        near = sum(
            lax.dot_general(
                part, choose, (((0,), (0,)), ((), ())), preferred_element_type=F32
            )
            for part in (high, middle, low)
        )
        cap = jnp.where(polar[mk * strips + strip] == 1, np.float32(NEG), np.float32(0.0))
        for gk in range(2):
            out_ref[:, 2 * mk + gk, :] = near * LOG2E + jnp.where(gq == gk, cap, np.float32(NEG))


def filter_line(x, r, lanes, taps_ref, shift_ref, land_ref, edge_ref, act_ref, rows, cols):
    sub = lax.broadcasted_iota(jnp.int32, (cols, 128), 0)
    tap = [[taps_ref[a, b : b + 1, lanes] for b in range(3)] for a in range(3)]
    y = [tap[0][b] * x[0] + tap[1][b] * x[1] + tap[2][b] * x[2] for b in range(3)]
    y0 = jnp.where(sub == 0, 0.0, pltpu.roll(y[0], 1, 0))
    y2 = jnp.where(sub == cols - 1, 0.0, pltpu.roll(y[2], cols - 1, 0))
    filtered = land_ref[r * cols : (r + 1) * cols] * shift_ref[:, lanes] + y[1] + (y0 + y2)
    edge_ref[r : r + 1, lanes] = filtered[0:1]
    edge_ref[rows + r : rows + r + 1, lanes] = filtered[cols - 1 : cols]
    act_ref[r * cols : (r + 1) * cols, lanes] = gelu(filtered).astype(BF16)


def spread_land(land, cols):
    rows = land.shape[0]
    tokens = rows * cols
    token = lax.broadcasted_iota(jnp.int32, (tokens, cols), 0)
    at = lax.broadcasted_iota(jnp.int32, (tokens, cols), 1)
    row_of = lax.broadcasted_iota(jnp.int32, (tokens, rows), 0) // cols
    pick_row = (row_of == lax.broadcasted_iota(jnp.int32, (tokens, rows), 1)).astype(F32)
    by_row = jnp.dot(pick_row, land.astype(F32), preferred_element_type=F32)
    mine = jnp.where(lax.rem(token, cols) == at, by_row, 0.0)
    return jnp.dot(mine, jnp.ones((cols, 128), F32), preferred_element_type=F32)


def inner_kernel(*refs, aliased, early, chunk):
    ins, refs = refs[:7], refs[7 + aliased :]
    outs, (rel_ref, polar_ref, sem) = refs[:-3], refs[-3:]
    e_ref, taps_ref, shift_ref, land_raw, w_hbm, rel_hbm, polar_hbm = ins
    act_ref, edge_ref, land_ref, w_ref, bias_ref = outs[:5]
    rows, cols, width_exp = e_ref.shape
    here = lax.axis_index("nlo") == 0

    @pl.when(here if early else ~here)
    def _():
        copies = [
            pltpu.make_async_copy(src, dst, sem.at[i])
            for i, (src, dst) in enumerate(
                (
                    (rel_hbm, rel_ref), (polar_hbm, polar_ref), (w_hbm, w_ref),
                )
            )
        ]
        for copy in copies:
            copy.start()
        land_ref[...] = spread_land(land_raw[...], cols)

        def step(i, carry):
            lanes = pl.ds(pl.multiple_of(i * 128, 128), 128)
            x = [e_ref[r, :, lanes].astype(F32) for r in range(rows)]
            for r in range(1, rows - 1):
                filter_line(
                    x[r - 1 : r + 2], r, lanes, taps_ref, shift_ref, land_ref, edge_ref, act_ref,
                    rows, cols,
                )
            return carry

        lax.fori_loop(0, width_exp // 128, step, 0)
        for copy in copies[:2]:
            copy.wait()
        fill_bias(polar_ref, rel_ref[...], bias_ref, rows // 2, "nhi")
        for copy in copies[2:]:
            copy.wait()


def mix_kernel(
    e_ref, ra_ref, rb_ref, taps_ref, shift_ref, land_ref, w_ref, stream_ref, qkv_hbm, out_hbm,
    act_in, edge_in, mixed_ref, sent_ref, act_ref, edge_ref, qkv_ref, wout_ref, perm_ref, sem,
    *, chunk, lat,
):
    rows, cols, width_exp = e_ref.shape
    tokens = rows * cols
    steps = width_exp // chunk
    lat_even = even(lat)
    copies = [
        pltpu.make_async_copy(src, dst, sem.at[i])
        for i, (src, dst) in enumerate(((qkv_hbm, qkv_ref), (out_hbm, wout_ref)))
    ]
    for copy in copies:
        copy.start()
    perm_ref[...] = send_matrix(rows, cols, False)

    def conv(i):
        for k in range(chunk // 128):
            lanes = pl.ds(pl.multiple_of(i * chunk + k * 128, 128), 128)
            ra = ra_ref[:, lanes].astype(F32)
            rb = rb_ref[:, lanes].astype(F32)
            top = [jnp.where(lat_even, rb, ra)] + [e_ref[r, :, lanes].astype(F32) for r in (0, 1)]
            bottom = [e_ref[r, :, lanes].astype(F32) for r in (rows - 2, rows - 1)]
            bottom += [jnp.where(lat_even, ra, rb)]
            for x, r in ((top, 0), (bottom, rows - 1)):
                filter_line(
                    x, r, lanes, taps_ref, shift_ref, land_ref, edge_ref, act_ref, rows, cols
                )

    def step(i, carry):
        conv(i)
        return carry

    lax.fori_loop(0, steps, step, 0)
    projected = jnp.dot(act_ref[...], w_ref[...], preferred_element_type=F32)
    mixed = (stream_ref[...].reshape(projected.shape).astype(F32) + projected).astype(BF16)
    mixed_ref[...] = mixed
    normed = normalize(mixed.astype(F32)).astype(BF16)
    sent = jnp.dot(perm_ref[...], normed, preferred_element_type=F32)
    for k in range(tokens // 4):
        sent_ref[k] = sent[4 * k : 4 * k + 4].astype(BF16)
    for copy in copies:
        copy.wait()


def edge_kernel(
    edge_ref, ca_ref, cb_ref, taps_ref, w_ref, stream_ref, sent_ref, inner_ref,
    mixed_ref, out_ref, act, cell_ref, *, lon, chunk,
):
    double, width_exp = edge_ref.shape
    rows = double // 2
    lon_even = even(lon)
    half = rows // 2
    part = width_exp // half
    ca, cb = ca_ref[:, width_exp:].astype(F32), cb_ref[:, width_exp:].astype(F32)
    for side, cells in enumerate((jnp.where(lon_even, cb, ca), jnp.where(lon_even, ca, cb))):
        for end in range(2):
            for k in range(half):
                at, row = 2 * side + end, half * end + k
                cell_ref[at : at + 1, part * k : part * (k + 1)] = cells[row : row + 1]
    for i in range(width_exp // chunk):
        lanes = slice(i * chunk, (i + 1) * chunk)
        ca = ca_ref[:, lanes].astype(F32)
        cb = cb_ref[:, lanes].astype(F32)
        beyond = []
        for side, own in enumerate((jnp.where(lon_even, cb, ca), jnp.where(lon_even, ca, cb))):
            above, below = (cell_ref[2 * side + end : 2 * side + end + 1, lanes] for end in range(2))
            column = jnp.concatenate([above, own, below], axis=0)
            beyond.append(
                sum(
                    taps_ref[a, 2 * side : 2 * side + 1, lanes] * column[a : a + rows]
                    for a in range(3)
                )
            )
        filtered = edge_ref[:, lanes] + jnp.concatenate(beyond, axis=0)
        act[:, lanes] = gelu(filtered).astype(BF16)
    projected = jnp.dot(act[...], w_ref[...], preferred_element_type=F32)
    cols = stream_ref.shape[1]
    first = jnp.concatenate([stream_ref[r, 0:1].astype(F32) for r in range(rows)], axis=0)
    last = jnp.concatenate([stream_ref[r, cols - 1 : cols].astype(F32) for r in range(rows)], axis=0)
    mixed = (jnp.concatenate([first, last], axis=0) + projected).astype(BF16)
    mixed = mixed.astype(F32)
    normed = normalize(mixed).astype(BF16).astype(F32)
    sub = lax.broadcasted_iota(jnp.int32, (cols, mixed.shape[1]), 0)
    for r in range(rows):
        part = slice(r * cols, (r + 1) * cols)
        inner = inner_ref[part].astype(F32)
        inner = jnp.where(sub == 0, mixed[r : r + 1], inner)
        inner = jnp.where(sub == cols - 1, mixed[rows + r : rows + r + 1], inner)
        mixed_ref[part] = inner.astype(BF16)
    out_ref[...] = sent_ref[...]
    pairs = cols // 2
    strips = rows // 2
    for s in range(strips):
        for side, c2 in ((0, 0), (1, pairs - 1)):
            k = s * pairs + c2
            old = sent_ref[k].astype(F32)
            keep = [old[0:1], old[1:2], old[2:3], old[3:4]]
            for m in range(2):
                at = side * rows + m * strips + s
                keep[2 * m + side] = normed[at : at + 1]
            out_ref[k] = jnp.concatenate(keep, axis=0).astype(BF16)


def attend_kernel(x_ref, w_ref, bias_ref, out_ref, x_buf, qk_buf, v_buf, o_buf, *, heads):
    tokens = 4 * x_ref.shape[0]
    width = x_ref.shape[2]
    head_dim = width // heads
    for k in range(tokens // 4):
        x_buf[4 * k : 4 * k + 4, :] = x_ref[k].astype(F32)
    x = x_buf[...].astype(BF16)
    scale = np.float32(head_dim**-0.5) * LOG2E
    per = 128 // head_dim
    lane_head = lax.broadcasted_iota(jnp.int32, (tokens, 128), 1) // head_dim
    ones = jnp.ones((16, tokens), BF16)
    both = 2 * width
    qk_buf[...] = jnp.dot(x, w_ref[:, :both], preferred_element_type=F32).astype(BF16)
    v_buf[...] = jnp.dot(x, w_ref[:, both:], preferred_element_type=F32)
    for p in range(heads // per):
        lanes = slice(128 * p, 128 * (p + 1))
        q = qk_buf[:, lanes]
        k = qk_buf[:, width + 128 * p : width + 128 * (p + 1)]
        v_t = jnp.concatenate([jnp.transpose(v_buf[:, lanes]).astype(BF16), ones], axis=0)
        queries = jnp.concatenate(
            [jnp.where(lane_head == j, q, jnp.zeros_like(q)) for j in range(per)], axis=0
        )
        scores = lax.dot_general(
            k, queries, (((1,), (1,)), ((), ())), preferred_element_type=F32
        )
        weights = []
        for j in range(per):
            base = bias_ref[p * per + j]
            bias = jnp.concatenate(
                [base if n == 0 else pltpu.roll(base, 16 * n, 1) for n in range(GRID)], axis=0
            )
            s = scores[:, tokens * j : tokens * (j + 1)] * scale + bias
            weights.append(jnp.exp2(s - jnp.max(s, axis=0, keepdims=True)).astype(BF16))
        summed = jnp.dot(v_t, jnp.concatenate(weights, axis=1), preferred_element_type=F32)
        parts = []
        for j in range(per):
            block = summed[:, tokens * j : tokens * (j + 1)]
            parts.append(block[head_dim * j : head_dim * (j + 1)] * (1.0 / block[128:129]))
        o_buf[:, lanes] = jnp.transpose(jnp.concatenate(parts, axis=0))
    for k in range(tokens // 4):
        out_ref[k] = o_buf[4 * k : 4 * k + 4, :].astype(BF16)


def out_kernel(a_ref, w_ref, mixed_ref, out_ref, a_buf, *, rows, cols):
    tokens = rows * cols
    for k in range(tokens // 4):
        a_buf[4 * k : 4 * k + 4, :] = a_ref[k].astype(F32)
    attended = jnp.dot(
        send_matrix(rows, cols, True), a_buf[...].astype(BF16), preferred_element_type=F32
    ).astype(BF16)
    result = mixed_ref[...].astype(F32) + jnp.dot(
        attended, w_ref[...], preferred_element_type=F32
    )
    out_ref[...] = result.astype(BF16)


def local(expanded, stream, land, polar, land_shift, dw_kernel, w_proj, w_qkv, w_out, rel_bias):
    rows, cols, width_exp = expanded.shape
    width = stream.shape[2]
    heads = rel_bias.shape[0]
    tokens = rows * cols
    lon, lat = ("nhi", "nlo"), "lat"
    lons, lats = lax.axis_size(lon), lax.axis_size(lat)
    everyone = lon + (lat,)
    swap_core = [(i, i ^ 1) for i in range(lats)]
    swap_next = [(i, j) for k in range(1, lats - 1, 2) for i, j in ((k, k + 1), (k + 1, k))]

    def call(kernel, name, ins, in_specs, outs, scratch, limit, **more):
        return pl.pallas_call(
            kernel,
            name=name,
            out_shape=tuple(pltpu.VMEM(shape, dtype) for shape, dtype in outs),
            in_specs=in_specs,
            out_specs=(VM,) * len(outs),
            scratch_shapes=scratch,
            compiler_params=pltpu.CompilerParams(vmem_limit_bytes=limit << 20),
            **more,
        )(*ins)

    row_shape, col_shape = ((cols, width_exp), BF16), ((rows, width_exp), BF16)
    end_shape = ((2, width_exp), BF16)
    small = (expanded, dw_kernel, land_shift[None], land, stream)
    e_here, taps, shift, land, stream, *picked = call(
        functools.partial(pick_kernel, lat=lat, lon=lon), "pick", map(in_hbm, small), [HBM] * 5,
        [(x.shape, x.dtype) for x in small] + [end_shape] * 2 + [row_shape] * 2 + [col_shape] * 2,
        [pltpu.VMEM((rows, width_exp), F32)] * 2 + [pltpu.SemaphoreType.DMA((rows + 4,))], 8,
    )
    rel = jnp.transpose(rel_bias, (1, 2, 0)).reshape(-1, heads)
    chunk = 256
    fixed = (e_here, taps, shift, land, *map(in_hbm, (w_proj, rel, polar)))
    inner_outs = [
        ((tokens, width_exp), BF16), ((2 * rows, width_exp), F32), ((tokens, 128), F32),
        (w_proj.shape, BF16), ((heads, 2 * GRID, 128), F32),
    ]
    inner_scratch = [
        pltpu.VMEM(rel.shape, F32), pltpu.SMEM(polar.shape, jnp.int32), pltpu.SemaphoreType.DMA((3,)),
    ]
    end_a, end_b, row_a, row_b, col_a, col_b = picked
    far_a = lax.ppermute(end_a, lat, swap_core)
    far_b = lax.ppermute(end_b, lat, swap_next)
    got_a = lax.ppermute(row_a, lat, swap_core)
    got_b = lax.ppermute(row_b, lat, swap_next)
    *inner, far_a = call(
        functools.partial(inner_kernel, aliased=1, early=True, chunk=chunk), "inner_early",
        (*fixed, far_a), [VM] * 4 + [HBM] * 3 + [VM],
        inner_outs + [end_shape], inner_scratch, 8, input_output_aliases={7: 5},
    )
    col_a, col_b = call(
        functools.partial(pack_kernel, lat=lat, lon=lon), "pack", (col_a, col_b, far_a, far_b),
        [VM] * 4, [((rows, width_exp + 2 * width_exp // rows), BF16)] * 2, [], 4,
    )
    seen_b = lax.ppermute(
        col_b, lon, [(i, (i + 1) % lons if i % 2 else (i - 1) % lons) for i in range(lons)]
    )
    seen_a = lax.ppermute(col_a, lon, [(i, i ^ 1) for i in range(lons)])
    act, edge, land_lanes, w_proj, bias, *_ = call(
        functools.partial(inner_kernel, aliased=6, early=False, chunk=chunk), "inner_late",
        (*fixed, *inner, col_a), [VM] * 4 + [HBM] * 3 + [VM] * 6, inner_outs, inner_scratch, 8,
        input_output_aliases={7 + i: i for i in range(5)},
        cost_estimate=pl.CostEstimate(flops=10**9, bytes_accessed=10**6, transcendentals=0),
    )
    token_shape, sent_shape = ((tokens, width), BF16), ((tokens // 4, 4, width), BF16)
    mixed, sent, act, edge, w_qkv, w_out = call(
        functools.partial(mix_kernel, chunk=chunk, lat=lat), "mix",
        (
            e_here, got_a, got_b, taps, shift, land_lanes, w_proj, stream,
            in_hbm(w_qkv), in_hbm(w_out), act, edge,
        ),
        [VM] * 8 + [HBM] * 2 + [VM] * 2,
        [token_shape, sent_shape] + inner_outs[:2] + [(w_qkv.shape, BF16), (w_out.shape, BF16)],
        [
            pltpu.VMEM((tokens, tokens), BF16), pltpu.SemaphoreType.DMA((2,)),
        ],
        8, input_output_aliases={10: 2, 11: 3},
        cost_estimate=pl.CostEstimate(flops=10**9, bytes_accessed=10**6, transcendentals=0),
    )
    mixed, sent = call(
        functools.partial(edge_kernel, lon=lon, chunk=chunk), "edge",
        (edge, seen_a, seen_b, taps, w_proj, stream, sent, mixed), [VM] * 8,
        [token_shape, sent_shape],
        [pltpu.VMEM((2 * rows, width_exp), BF16), pltpu.VMEM((4, width_exp), F32)], 8,
    )

    group = ("nhi", lat)
    mine = lax.all_to_all(sent, group, 0, 0, tiled=True)
    attended = pl.pallas_call(
        functools.partial(attend_kernel, heads=heads),
        name="attend",
        out_shape=jax.ShapeDtypeStruct((tokens // 4, 4, width), BF16),
        in_specs=[VM] * 3,
        out_specs=VM,
        scratch_shapes=[
            pltpu.VMEM((tokens, width), F32), pltpu.VMEM((tokens, 2 * width), BF16),
            pltpu.VMEM((tokens, width), F32), pltpu.VMEM((tokens, width), F32),
        ],
        compiler_params=pltpu.CompilerParams(vmem_limit_bytes=8 << 20),
    )(mine, w_qkv, bias)
    back = lax.all_to_all(attended, group, 0, 0, tiled=True)
    result = pl.pallas_call(
        functools.partial(out_kernel, rows=rows, cols=cols),
        name="out",
        out_shape=jax.ShapeDtypeStruct((tokens, width), BF16),
        in_specs=[VM] * 3,
        out_specs=VM,
        scratch_shapes=[pltpu.VMEM((tokens, width), F32)],
        compiler_params=pltpu.CompilerParams(vmem_limit_bytes=8 << 20),
    )(back, w_out, mixed)
    return result.reshape(rows, cols, width)


def solution(mesh):
    lons, lats = mesh.shape["lon"], mesh.shape["lat"]
    fine = Mesh(mesh.devices.reshape(GRID, lons // GRID, lats), ("nhi", "nlo", "lat"))
    lon = ("nhi", "nlo")
    in_specs = (P("lat", lon, None), P("lat", lon, None), P("lat", lon)) + (P(),) * 7
    return jax.shard_map(
        local, mesh=fine, in_specs=in_specs, out_specs=P("lat", lon, None), check_vma=False
    )
```

```python
import functools

import jax
import jax.numpy as jnp
import numpy as np
from jax import lax
from jax.experimental import pallas as pl
from jax.experimental.pallas import tpu as pltpu
from jax.sharding import Mesh
from jax.sharding import PartitionSpec as P

GRID = 8
EPS = 1e-05
NEG = -1e30
LOG2E = np.float32(np.log2(np.e))
F32 = jnp.float32
BF16 = jnp.bfloat16
VM = pl.BlockSpec(memory_space=pltpu.VMEM)
SM = pl.BlockSpec(memory_space=pltpu.SMEM)
HBM = pl.BlockSpec(memory_space=pltpu.HBM)


def at_pole(lat):
    at = lax.axis_index(lat)
    return (at == 0) | (at == lax.axis_size(lat) - 1)


def in_hbm(x):
    return pltpu.with_memory_space_constraint(x, pltpu.HBM)


def send_matrix(rows, cols):
    tokens = rows * cols
    strips, pairs = rows // 2, cols // 2
    to = lax.broadcasted_iota(jnp.int32, (tokens, tokens), 0)
    at = lax.broadcasted_iota(jnp.int32, (tokens, tokens), 1)
    s, rest = to // (4 * pairs), to % (4 * pairs)
    c2, m, c1 = rest // 4, rest % 4 // 2, rest % 2
    token = (m * strips + s) * cols + 2 * c2 + c1
    return jnp.where(token == at, 1.0, 0.0).astype(BF16)


def even(axes):
    return lax.rem(lax.axis_index(axes), 2) == 0


def pick_kernel(*refs, lat, lon):
    ins, outs, refs = refs[:5], refs[5:10], refs[10:]
    xa_ref, xb_ref, ra_ref, rb_ref, ca_ref, cb_ref, first, last, sem = refs
    e_hbm, e_ref = ins[0], outs[0]
    rows, cols, _ = e_ref.shape
    lines = [pltpu.make_async_copy(e_hbm.at[r], e_ref.at[r], sem.at[r]) for r in range(rows)]
    rest = [
        pltpu.make_async_copy(src, dst, sem.at[rows + i])
        for i, (src, dst) in enumerate(zip(ins[1:], outs[1:]))
    ]
    for copy in lines + rest:
        copy.start()
    for r in range(rows):
        lines[r].wait()
        line = e_ref[r].astype(F32)
        first[r : r + 1, :] = line[0:1]
        last[r : r + 1, :] = line[cols - 1 : cols]
    lat_even, lon_even = even(lat), even(lon)
    top = e_ref[0].astype(F32)
    bottom = e_ref[rows - 1].astype(F32)
    ra_ref[...] = jnp.where(lat_even, bottom, top).astype(BF16)
    rb_ref[...] = jnp.where(lat_even, top, bottom).astype(BF16)
    a, b = first[...], last[...]
    ca_ref[...] = jnp.where(lon_even, b, a).astype(BF16)
    cb_ref[...] = jnp.where(lon_even, a, b).astype(BF16)
    above = jnp.concatenate([a[0:1], b[0:1]], axis=0)
    below = jnp.concatenate([a[rows - 1 : rows], b[rows - 1 : rows]], axis=0)
    xa_ref[...] = jnp.where(lat_even, below, above).astype(BF16)
    xb_ref[...] = jnp.where(lat_even, above, below).astype(BF16)
    for copy in rest:
        copy.wait()


def pack_kernel(c_ref, xa_ref, xb_ref, taps_ref, *refs, lat, lon, second):
    o_ref = refs[-1]
    lat_even, is_last = even(lat), even(lon) ^ second
    rows = c_ref.shape[0]
    xa, xb = xa_ref[...].astype(F32), jnp.where(at_pole(lat), 0.0, xb_ref[...].astype(F32))
    above, below = jnp.where(lat_even, xb, xa), jnp.where(lat_even, xa, xb)
    sub = lax.broadcasted_iota(jnp.int32, c_ref.shape, 0)
    here = c_ref[...].astype(F32)
    up, down = (jnp.where(is_last, end[1:2], end[0:1]) for end in (above, below))
    up = jnp.where(sub == 0, up, pltpu.roll(here, 1, 0))
    down = jnp.where(sub == rows - 1, down, pltpu.roll(here, rows - 1, 0))
    tap = [jnp.where(is_last, taps_ref[i, 0:1], taps_ref[i, 2:3]) for i in range(3)]
    o_ref[...] = (tap[0] * up + tap[1] * here + tap[2] * down).astype(BF16)


def gelu(x):
    inner = x * (np.float32(np.sqrt(2 / np.pi)) + np.float32(0.044715 * np.sqrt(2 / np.pi)) * (x * x))
    half = np.float32(0.5) * x
    return half + half * jnp.tanh(inner)


def normalize(flat):
    centred = flat - jnp.mean(flat, axis=1, keepdims=True)
    spread = jnp.mean(centred * centred, axis=1, keepdims=True)
    return centred * lax.rsqrt(spread + EPS)


def fill_bias(polar, rel, out_ref, strips, nhi):
    strip = lax.axis_index(nhi) * strips // lax.axis_size(nhi)
    high = rel.astype(BF16)
    middle = (rel - high.astype(F32)).astype(BF16)
    low = (rel - high.astype(F32) - middle.astype(F32)).astype(BF16)
    offsets = rel.shape[0]
    lane = lax.broadcasted_iota(jnp.int32, (offsets, 128), 1)
    mq = lane // 2 % GRID
    nq = lane // (2 * GRID)
    at = lax.broadcasted_iota(jnp.int32, (offsets, 128), 0)
    gq = lax.broadcasted_iota(jnp.int32, (1, 128), 1) % 2
    for mk in range(GRID):
        wanted = (mk - mq + GRID - 1) * GRID + (GRID - nq) % GRID
        choose = jnp.where(at == wanted, 1.0, 0.0).astype(BF16)
        near = sum(
            lax.dot_general(
                part, choose, (((0,), (0,)), ((), ())), preferred_element_type=F32
            )
            for part in (high, middle, low)
        )
        cap = jnp.where(polar[mk * strips + strip] == 1, np.float32(NEG), np.float32(0.0))
        for gk in range(2):
            out_ref[:, 2 * mk + gk, :] = near * LOG2E + jnp.where(gq == gk, cap, np.float32(NEG))


def filter_line(x, r, lanes, taps_ref, shift_ref, land_ref, edge_ref, act_ref, rows, cols):
    sub = lax.broadcasted_iota(jnp.int32, (cols, 128), 0)
    tap = [[taps_ref[a, b : b + 1, lanes] for b in range(3)] for a in range(3)]
    y = [tap[0][b] * x[0] + tap[1][b] * x[1] + tap[2][b] * x[2] for b in range(3)]
    y0 = jnp.where(sub == 0, 0.0, pltpu.roll(y[0], 1, 0))
    y2 = jnp.where(sub == cols - 1, 0.0, pltpu.roll(y[2], cols - 1, 0))
    filtered = land_ref[r * cols : (r + 1) * cols] * shift_ref[:, lanes] + y[1] + (y0 + y2)
    edge_ref[r : r + 1, lanes] = filtered[0:1]
    edge_ref[rows + r : rows + r + 1, lanes] = filtered[cols - 1 : cols]
    act_ref[r * cols : (r + 1) * cols, lanes] = gelu(filtered).astype(BF16)


def spread_land(land, cols):
    rows = land.shape[0]
    tokens = rows * cols
    token = lax.broadcasted_iota(jnp.int32, (tokens, cols), 0)
    at = lax.broadcasted_iota(jnp.int32, (tokens, cols), 1)
    row_of = lax.broadcasted_iota(jnp.int32, (tokens, rows), 0) // cols
    pick_row = (row_of == lax.broadcasted_iota(jnp.int32, (tokens, rows), 1)).astype(F32)
    by_row = jnp.dot(pick_row, land.astype(F32), preferred_element_type=F32)
    mine = jnp.where(lax.rem(token, cols) == at, by_row, 0.0)
    return jnp.dot(mine, jnp.ones((cols, 128), F32), preferred_element_type=F32)


def inner_kernel(*refs, aliased, early, chunk):
    ins, refs = refs[:7], refs[7 + aliased :]
    outs, (rel_ref, polar_ref, sem) = refs[:-3], refs[-3:]
    e_ref, taps_ref, shift_ref, land_raw, w_hbm, rel_hbm, polar_hbm = ins
    act_ref, edge_ref, land_ref, w_ref, bias_ref = outs[:5]
    rows, cols, width_exp = e_ref.shape
    here = lax.axis_index("nlo") == 0

    @pl.when(here if early else ~here)
    def _():
        copies = [
            pltpu.make_async_copy(src, dst, sem.at[i])
            for i, (src, dst) in enumerate(
                (
                    (rel_hbm, rel_ref), (polar_hbm, polar_ref), (w_hbm, w_ref),
                )
            )
        ]
        for copy in copies:
            copy.start()
        land_ref[...] = spread_land(land_raw[...], cols)

        def step(i, carry):
            lanes = pl.ds(pl.multiple_of(i * 128, 128), 128)
            x = [e_ref[r, :, lanes].astype(F32) for r in range(rows)]
            for r in range(1, rows - 1):
                filter_line(
                    x[r - 1 : r + 2], r, lanes, taps_ref, shift_ref, land_ref, edge_ref, act_ref,
                    rows, cols,
                )
            return carry

        lax.fori_loop(0, width_exp // 128, step, 0)
        for copy in copies[:2]:
            copy.wait()
        fill_bias(polar_ref, rel_ref[...], bias_ref, rows // 2, "nhi")
        for copy in copies[2:]:
            copy.wait()


def mix_kernel(
    e_ref, ra_ref, rb_ref, taps_ref, shift_ref, land_ref, w_ref, stream_ref, qkv_hbm, out_hbm,
    act_in, edge_in, mixed_ref, sent_ref, act_ref, edge_ref, qkv_ref, wout_ref, perm_ref, sem,
    *, chunk, lat,
):
    rows, cols, width_exp = e_ref.shape
    tokens = rows * cols
    steps = width_exp // chunk
    lat_even, pole = even(lat), at_pole(lat)
    copies = [
        pltpu.make_async_copy(src, dst, sem.at[i])
        for i, (src, dst) in enumerate(((qkv_hbm, qkv_ref), (out_hbm, wout_ref)))
    ]
    for copy in copies:
        copy.start()
    perm_ref[...] = send_matrix(rows, cols)

    def conv(i):
        for k in range(chunk // 128):
            lanes = pl.ds(pl.multiple_of(i * chunk + k * 128, 128), 128)
            ra = ra_ref[:, lanes].astype(F32)
            rb = jnp.where(pole, 0.0, rb_ref[:, lanes].astype(F32))
            top = [jnp.where(lat_even, rb, ra)] + [e_ref[r, :, lanes].astype(F32) for r in (0, 1)]
            bottom = [e_ref[r, :, lanes].astype(F32) for r in (rows - 2, rows - 1)]
            bottom += [jnp.where(lat_even, ra, rb)]
            for x, r in ((top, 0), (bottom, rows - 1)):
                filter_line(
                    x, r, lanes, taps_ref, shift_ref, land_ref, edge_ref, act_ref, rows, cols
                )

    def step(i, carry):
        conv(i)
        return carry

    lax.fori_loop(0, steps, step, 0)
    projected = jnp.dot(act_ref[...], w_ref[...], preferred_element_type=F32)
    mixed = (stream_ref[...].reshape(projected.shape).astype(F32) + projected).astype(BF16)
    mixed_ref[...] = mixed
    normed = normalize(mixed.astype(F32)).astype(BF16)
    sent = jnp.dot(perm_ref[...], normed, preferred_element_type=F32)
    for k in range(tokens // 4):
        sent_ref[k] = sent[4 * k : 4 * k + 4].astype(BF16)
    for copy in copies:
        copy.wait()


def edge_kernel(
    edge_ref, ca_ref, cb_ref, w_ref, stream_ref, sent_ref, inner_ref, mixed_ref, out_ref,
    *, lon, chunk,
):
    double, width_exp = edge_ref.shape
    rows = double // 2
    lon_even = even(lon)
    projected = 0.0
    for at in range(0, width_exp, chunk):
        lanes = slice(at, at + chunk)
        ca, cb = ca_ref[:, lanes].astype(F32), cb_ref[:, lanes].astype(F32)
        beyond = jnp.where(lon_even, cb, ca), jnp.where(lon_even, ca, cb)
        act = gelu(edge_ref[:, lanes] + jnp.concatenate(beyond, axis=0)).astype(BF16)
        projected += jnp.dot(act, w_ref[lanes, :], preferred_element_type=F32)
    cols = stream_ref.shape[1]
    first = jnp.concatenate([stream_ref[r, 0:1].astype(F32) for r in range(rows)], axis=0)
    last = jnp.concatenate([stream_ref[r, cols - 1 : cols].astype(F32) for r in range(rows)], axis=0)
    mixed = (jnp.concatenate([first, last], axis=0) + projected).astype(BF16)
    mixed = mixed.astype(F32)
    normed = normalize(mixed).astype(BF16).astype(F32)
    sub = lax.broadcasted_iota(jnp.int32, (cols, mixed.shape[1]), 0)
    for r in range(rows):
        part = slice(r * cols, (r + 1) * cols)
        inner = inner_ref[part].astype(F32)
        inner = jnp.where(sub == 0, mixed[r : r + 1], inner)
        inner = jnp.where(sub == cols - 1, mixed[rows + r : rows + r + 1], inner)
        mixed_ref[part] = inner.astype(BF16)
    pairs = cols // 2
    strips = rows // 2
    for s in range(strips):
        for side, c2 in ((0, 0), (1, pairs - 1)):
            k = s * pairs + c2
            old = sent_ref[k].astype(F32)
            keep = [old[0:1], old[1:2], old[2:3], old[3:4]]
            for m in range(2):
                at = side * rows + m * strips + s
                keep[2 * m + side] = normed[at : at + 1]
            out_ref[k] = jnp.concatenate(keep, axis=0).astype(BF16)


def attend_kernel(x_ref, w_ref, bias_ref, out_ref, x_buf, qk_buf, v_buf, s_buf, p_buf, t_buf, *, heads):
    tokens = 4 * x_ref.shape[0]
    width = x_ref.shape[2]
    head_dim = width // heads
    for k in range(tokens // 4):
        x_buf[4 * k : 4 * k + 4, :] = x_ref[k].astype(F32)
    x = x_buf[...].astype(BF16)
    scale = np.float32(head_dim**-0.5) * LOG2E
    per = 128 // head_dim
    packs = heads // per
    row_head = lax.broadcasted_iota(jnp.int32, (128, tokens), 0) // head_dim
    ones = jnp.ones((16, tokens), BF16)
    both = 2 * width
    qk_buf[...] = jnp.dot(x, w_ref[:, :both], preferred_element_type=F32).astype(BF16)
    v_buf[...] = jnp.dot(x, w_ref[:, both:], preferred_element_type=F32).astype(BF16)
    for p in range(packs):
        q = jnp.transpose(qk_buf[:, 128 * p : 128 * (p + 1)])
        queries = jnp.concatenate(
            [jnp.where(row_head == j, q, jnp.zeros_like(q)) for j in range(per)], axis=1
        )
        keys = qk_buf[:, width + 128 * p : width + 128 * (p + 1)]
        span = slice(per * tokens * p, per * tokens * (p + 1))
        s_buf[:, span] = jnp.dot(keys, queries, preferred_element_type=F32)
    for h in range(heads):
        base = bias_ref[h]
        bias = jnp.concatenate(
            [base if n == 0 else pltpu.roll(base, 2 * GRID * n, 1) for n in range(GRID)], axis=0
        )
        span = slice(tokens * h, tokens * (h + 1))
        s = s_buf[:, span] * scale + bias
        p_buf[:, span] = jnp.exp2(s - jnp.max(s, axis=0, keepdims=True)).astype(BF16)
    for p in range(packs):
        values = jnp.concatenate([jnp.transpose(v_buf[:, 128 * p : 128 * (p + 1)]), ones], axis=0)
        span = slice(per * tokens * p, per * tokens * (p + 1))
        summed = jnp.dot(values, p_buf[:, span], preferred_element_type=F32)
        for j in range(per):
            block = summed[:, tokens * j : tokens * (j + 1)]
            at = 128 * p + head_dim * j
            t_buf[at : at + head_dim, :] = block[head_dim * j : head_dim * (j + 1)] * (
                1.0 / block[128:129]
            )
    for p in range(packs):
        x_buf[:, 128 * p : 128 * (p + 1)] = jnp.transpose(t_buf[128 * p : 128 * (p + 1), :])
    for k in range(tokens // 4):
        out_ref[k] = x_buf[4 * k : 4 * k + 4, :].astype(BF16)


def out_kernel(a_ref, w_ref, mixed_ref, out_ref, a_buf, *, rows, cols):
    strips, pairs = rows // 2, cols // 2
    for k in range(a_ref.shape[0]):
        got = a_ref[k].astype(F32)
        for m in range(2):
            at = (m * strips + k // pairs) * cols + 2 * (k % pairs)
            a_buf[at : at + 2, :] = got[2 * m : 2 * m + 2]
    result = mixed_ref[...].astype(F32) + jnp.dot(
        a_buf[...].astype(BF16), w_ref[...], preferred_element_type=F32
    )
    out_ref[...] = result.astype(BF16)


def local(expanded, stream, land, polar, land_shift, dw_kernel, w_proj, w_qkv, w_out, rel_bias):
    rows, cols, width_exp = expanded.shape
    width = stream.shape[2]
    heads = rel_bias.shape[0]
    tokens = rows * cols
    lon, lat = ("nhi", "nlo"), "lat"
    lons, lats = lax.axis_size(lon), lax.axis_size(lat)
    everyone = lon + (lat,)
    swap_core = [(i, i ^ 1) for i in range(lats)]
    swap_next = [(i, (i + 1) % lats if i % 2 else (i - 1) % lats) for i in range(lats)]

    def call(kernel, name, ins, in_specs, outs, scratch, limit, **more):
        return pl.pallas_call(
            kernel,
            name=name,
            out_shape=tuple(pltpu.VMEM(shape, dtype) for shape, dtype in outs),
            in_specs=in_specs,
            out_specs=(VM,) * len(outs),
            scratch_shapes=scratch,
            compiler_params=pltpu.CompilerParams(vmem_limit_bytes=limit << 20),
            **more,
        )(*ins)

    row_shape, col_shape = ((cols, width_exp), BF16), ((rows, width_exp), BF16)
    end_shape = ((2, width_exp), BF16)
    small = (expanded, dw_kernel, land_shift[None], land, stream)
    e_here, taps, shift, land, stream, *picked = call(
        functools.partial(pick_kernel, lat=lat, lon=lon), "pick", map(in_hbm, small), [HBM] * 5,
        [(x.shape, x.dtype) for x in small] + [end_shape] * 2 + [row_shape] * 2 + [col_shape] * 2,
        [pltpu.VMEM((rows, width_exp), F32)] * 2 + [pltpu.SemaphoreType.DMA((rows + 4,))], 8,
    )
    rel = jnp.transpose(rel_bias, (1, 2, 0)).reshape(-1, heads)
    chunk = 256
    fixed = (e_here, taps, shift, land, *map(in_hbm, (w_proj, rel, polar)))
    inner_outs = [
        ((tokens, width_exp), BF16), ((2 * rows, width_exp), F32), ((tokens, 128), F32),
        (w_proj.shape, BF16), ((heads, 2 * GRID, 128), F32),
    ]
    inner_scratch = [
        pltpu.VMEM(rel.shape, F32), pltpu.SMEM(polar.shape, jnp.int32), pltpu.SemaphoreType.DMA((3,)),
    ]
    end_a, end_b, row_a, row_b, col_a, col_b = picked
    far_a = lax.ppermute(end_a, lat, swap_core)
    far_b = lax.ppermute(end_b, lat, swap_next)
    got_a = lax.ppermute(row_a, lat, swap_core)
    got_b = lax.ppermute(row_b, lat, swap_next)
    *inner, far_a = call(
        functools.partial(inner_kernel, aliased=1, early=True, chunk=chunk), "inner_early",
        (*fixed, far_a), [VM] * 4 + [HBM] * 3 + [VM],
        inner_outs + [end_shape], inner_scratch, 8, input_output_aliases={7: 5},
    )
    packed = []
    for second, column in enumerate((col_a, col_b)):
        packed += call(
            functools.partial(pack_kernel, lat=lat, lon=lon, second=bool(second)), "pack",
            (column, far_a, far_b, taps, *packed), [VM] * (4 + second), [col_shape], [], 4,
        )
    col_a, col_b = packed
    seen_a = lax.ppermute(col_a, lon, [(i, i ^ 1) for i in range(lons)])
    seen_b = lax.ppermute(
        col_b, lon, [(i, (i + 1) % lons if i % 2 else (i - 1) % lons) for i in range(lons)]
    )
    act, edge, land_lanes, w_proj, bias, *_ = call(
        functools.partial(inner_kernel, aliased=6, early=False, chunk=chunk), "inner_late",
        (*fixed, *inner, col_a), [VM] * 4 + [HBM] * 3 + [VM] * 6, inner_outs, inner_scratch, 8,
        input_output_aliases={7 + i: i for i in range(5)},
        cost_estimate=pl.CostEstimate(flops=10**9, bytes_accessed=10**6, transcendentals=0),
    )
    token_shape, sent_shape = ((tokens, width), BF16), ((tokens // 4, 4, width), BF16)
    mixed, sent, act, edge, w_qkv, w_out = call(
        functools.partial(mix_kernel, chunk=chunk, lat=lat), "mix",
        (
            e_here, got_a, got_b, taps, shift, land_lanes, w_proj, stream,
            in_hbm(w_qkv), in_hbm(w_out), act, edge,
        ),
        [VM] * 8 + [HBM] * 2 + [VM] * 2,
        [token_shape, sent_shape] + inner_outs[:2] + [(w_qkv.shape, BF16), (w_out.shape, BF16)],
        [
            pltpu.VMEM((tokens, tokens), BF16), pltpu.SemaphoreType.DMA((2,)),
        ],
        8, input_output_aliases={10: 2, 11: 3},
        cost_estimate=pl.CostEstimate(flops=10**9, bytes_accessed=10**6, transcendentals=0),
    )
    mixed, sent = call(
        functools.partial(edge_kernel, lon=lon, chunk=width), "edge",
        (edge, seen_a, seen_b, w_proj, stream, sent, mixed), [VM] * 7,
        [token_shape, sent_shape], [], 8, input_output_aliases={5: 1, 6: 0},
    )

    group = ("nhi", lat)
    mine = lax.all_to_all(sent, group, 0, 0, tiled=True)
    attended = pl.pallas_call(
        functools.partial(attend_kernel, heads=heads),
        name="attend",
        out_shape=jax.ShapeDtypeStruct((tokens // 4, 4, width), BF16),
        in_specs=[VM] * 3,
        out_specs=VM,
        scratch_shapes=[
            pltpu.VMEM((tokens, width), F32), pltpu.VMEM((tokens, 2 * width), BF16),
            pltpu.VMEM((tokens, width), BF16), pltpu.VMEM((tokens, tokens * heads), F32),
            pltpu.VMEM((tokens, tokens * heads), BF16), pltpu.VMEM((width, tokens), F32),
        ],
        compiler_params=pltpu.CompilerParams(vmem_limit_bytes=8 << 20),
    )(mine, w_qkv, bias)
    back = lax.all_to_all(attended, group, 0, 0, tiled=True)
    result = pl.pallas_call(
        functools.partial(out_kernel, rows=rows, cols=cols),
        name="out",
        out_shape=jax.ShapeDtypeStruct((tokens, width), BF16),
        in_specs=[VM] * 3,
        out_specs=VM,
        scratch_shapes=[pltpu.VMEM((tokens, width), F32)],
        compiler_params=pltpu.CompilerParams(vmem_limit_bytes=8 << 20),
    )(back, w_out, mixed)
    return result.reshape(rows, cols, width)


def solution(mesh):
    lons, lats = mesh.shape["lon"], mesh.shape["lat"]
    fine = Mesh(mesh.devices.reshape(GRID, lons // GRID, lats), ("nhi", "nlo", "lat"))
    lon = ("nhi", "nlo")
    in_specs = (P("lat", lon, None), P("lat", lon, None), P("lat", lon)) + (P(),) * 7
    return jax.shard_map(
        local, mesh=fine, in_specs=in_specs, out_specs=P("lat", lon, None), check_vma=False
    )
```

```python
import functools

import jax
import jax.numpy as jnp
import numpy as np
from jax import lax
from jax.experimental import pallas as pl
from jax.experimental.pallas import tpu as pltpu
from jax.sharding import Mesh
from jax.sharding import PartitionSpec as P

GRID = 8
EPS = 1e-05
NEG = -1e30
LOG2E = np.float32(np.log2(np.e))
F32 = jnp.float32
BF16 = jnp.bfloat16
VM = pl.BlockSpec(memory_space=pltpu.VMEM)
SM = pl.BlockSpec(memory_space=pltpu.SMEM)
HBM = pl.BlockSpec(memory_space=pltpu.HBM)


def at_pole(lat):
    at = lax.axis_index(lat)
    return (at == 0) | (at == lax.axis_size(lat) - 1)


def in_hbm(x):
    return pltpu.with_memory_space_constraint(x, pltpu.HBM)


def send_matrix(rows, cols):
    tokens = rows * cols
    strips, pairs = rows // 2, cols // 2
    to = lax.broadcasted_iota(jnp.int32, (tokens, tokens), 0)
    at = lax.broadcasted_iota(jnp.int32, (tokens, tokens), 1)
    s, rest = to // (4 * pairs), to % (4 * pairs)
    c2, m, c1 = rest // 4, rest % 4 // 2, rest % 2
    token = (m * strips + s) * cols + 2 * c2 + c1
    return jnp.where(token == at, 1.0, 0.0).astype(BF16)


def even(axes):
    return lax.rem(lax.axis_index(axes), 2) == 0


def pick_kernel(*refs, lat):
    ins, outs, (xa_ref, xb_ref, ra_ref, rb_ref, first, last, sem) = refs[:4], refs[4:8], refs[8:]
    e_ref = outs[0]
    rows, cols, _ = e_ref.shape
    copies = [
        pltpu.make_async_copy(src, dst, sem.at[i]) for i, (src, dst) in enumerate(zip(ins, outs))
    ]
    for copy in copies:
        copy.start()
    lat_even = even(lat)
    copies[0].wait()
    ra_ref[...] = jnp.where(lat_even, e_ref[rows - 1], e_ref[0])
    rb_ref[...] = jnp.where(lat_even, e_ref[0], e_ref[rows - 1])
    lines = [e_ref[r].astype(F32) for r in range(rows)]
    a = jnp.concatenate([line[0:1] for line in lines], axis=0)
    b = jnp.concatenate([line[cols - 1 : cols] for line in lines], axis=0)
    first[...] = a.astype(BF16)
    last[...] = b.astype(BF16)
    above = jnp.concatenate([a[0:1], b[0:1]], axis=0)
    below = jnp.concatenate([a[rows - 1 : rows], b[rows - 1 : rows]], axis=0)
    xa_ref[...] = jnp.where(lat_even, below, above).astype(BF16)
    xb_ref[...] = jnp.where(lat_even, above, below).astype(BF16)
    for copy in copies[1:]:
        copy.wait()


def pack_kernel(c_ref, xa_ref, xb_ref, taps_ref, *refs, lat, is_last):
    o_ref = refs[-1]
    lat_even = even(lat)
    rows = c_ref.shape[0]
    end, tap = (1, 0) if is_last else (0, 2)
    xa, xb = (ref[end : end + 1].astype(F32) for ref in (xa_ref, xb_ref))
    xb = jnp.where(at_pole(lat), 0.0, xb)
    above, below = jnp.where(lat_even, xb, xa), jnp.where(lat_even, xa, xb)
    sub = lax.broadcasted_iota(jnp.int32, c_ref.shape, 0)
    here = c_ref[...].astype(F32)
    above = jnp.where(sub == 0, above, pltpu.roll(here, 1, 0))
    below = jnp.where(sub == rows - 1, below, pltpu.roll(here, rows - 1, 0))
    tap = [taps_ref[i, tap : tap + 1] for i in range(3)]
    o_ref[...] = (tap[0] * above + tap[1] * here + tap[2] * below).astype(BF16)


def gelu(x):
    inner = x * (np.float32(np.sqrt(2 / np.pi)) + np.float32(0.044715 * np.sqrt(2 / np.pi)) * (x * x))
    half = np.float32(0.5) * x
    return half + half * jnp.tanh(inner)


def normalize(flat):
    centred = flat - jnp.mean(flat, axis=1, keepdims=True)
    spread = jnp.mean(centred * centred, axis=1, keepdims=True)
    return centred * lax.rsqrt(spread + EPS)


def fill_bias(polar, rel, out_ref, strips, nhi):
    strip = lax.axis_index(nhi) * strips // lax.axis_size(nhi)
    high = rel.astype(BF16)
    middle = (rel - high.astype(F32)).astype(BF16)
    low = (rel - high.astype(F32) - middle.astype(F32)).astype(BF16)
    offsets = rel.shape[0]
    lane = lax.broadcasted_iota(jnp.int32, (offsets, 128), 1)
    mq = lane // 2 % GRID
    nq = lane // (2 * GRID)
    at = lax.broadcasted_iota(jnp.int32, (offsets, 128), 0)
    gq = lax.broadcasted_iota(jnp.int32, (1, 128), 1) % 2
    for mk in range(GRID):
        wanted = (mk - mq + GRID - 1) * GRID + (GRID - nq) % GRID
        choose = jnp.where(at == wanted, 1.0, 0.0).astype(BF16)
        near = sum(
            lax.dot_general(
                part, choose, (((0,), (0,)), ((), ())), preferred_element_type=F32
            )
            for part in (high, middle, low)
        )
        cap = jnp.where(polar[mk * strips + strip] == 1, np.float32(NEG), np.float32(0.0))
        for gk in range(2):
            out_ref[:, 2 * mk + gk, :] = near * LOG2E + jnp.where(gq == gk, cap, np.float32(NEG))


def filter_line(x, r, lanes, taps_ref, shift_ref, land_ref, edge_ref, act_ref, rows, cols):
    sub = lax.broadcasted_iota(jnp.int32, (cols, 128), 0)
    tap = [[taps_ref[a, b : b + 1, lanes] for b in range(3)] for a in range(3)]
    y = [tap[0][b] * x[0] + tap[1][b] * x[1] + tap[2][b] * x[2] for b in range(3)]
    y0 = jnp.where(sub == 0, 0.0, pltpu.roll(y[0], 1, 0))
    y2 = jnp.where(sub == cols - 1, 0.0, pltpu.roll(y[2], cols - 1, 0))
    filtered = land_ref[r * cols : (r + 1) * cols] * shift_ref[:, lanes] + y[1] + (y0 + y2)
    edge_ref[r : r + 1, lanes] = filtered[0:1]
    edge_ref[rows + r : rows + r + 1, lanes] = filtered[cols - 1 : cols]
    act_ref[r * cols : (r + 1) * cols, lanes] = gelu(filtered).astype(BF16)


def spread_land(land, cols):
    rows = land.shape[0]
    tokens = rows * cols
    token = lax.broadcasted_iota(jnp.int32, (tokens, cols), 0)
    at = lax.broadcasted_iota(jnp.int32, (tokens, cols), 1)
    row_of = lax.broadcasted_iota(jnp.int32, (tokens, rows), 0) // cols
    pick_row = (row_of == lax.broadcasted_iota(jnp.int32, (tokens, rows), 1)).astype(F32)
    by_row = jnp.dot(pick_row, land.astype(F32), preferred_element_type=F32)
    mine = jnp.where(lax.rem(token, cols) == at, by_row, 0.0)
    return jnp.dot(mine, jnp.ones((cols, 128), F32), preferred_element_type=F32)


def inner_kernel(*refs, aliased, early, chunk):
    ins, refs = refs[:8], refs[8 + aliased :]
    outs, (rel_ref, polar_ref, sem) = refs[:-3], refs[-3:]
    e_ref, taps_ref, shift_ref, land_raw, w_hbm, rel_hbm, polar_hbm, stream_hbm = ins
    act_ref, edge_ref, land_ref, w_ref, bias_ref, stream_ref = outs[:6]
    rows, cols, width_exp = e_ref.shape
    here = lax.axis_index("nlo") == 0

    @pl.when(here if early else ~here)
    def _():
        copies = [
            pltpu.make_async_copy(src, dst, sem.at[i])
            for i, (src, dst) in enumerate(
                (
                    (rel_hbm, rel_ref), (polar_hbm, polar_ref), (w_hbm, w_ref),
                    (stream_hbm, stream_ref),
                )
            )
        ]
        for copy in copies:
            copy.start()
        land_ref[...] = spread_land(land_raw[...], cols)

        def step(i, carry):
            lanes = pl.ds(pl.multiple_of(i * 128, 128), 128)
            x = [e_ref[r, :, lanes].astype(F32) for r in range(rows)]
            for r in range(1, rows - 1):
                filter_line(
                    x[r - 1 : r + 2], r, lanes, taps_ref, shift_ref, land_ref, edge_ref, act_ref,
                    rows, cols,
                )
            return carry

        lax.fori_loop(0, width_exp // 128, step, 0)
        for copy in copies[:2]:
            copy.wait()
        fill_bias(polar_ref, rel_ref[...], bias_ref, rows // 2, "nhi")
        for copy in copies[2:]:
            copy.wait()


def mix_kernel(
    e_ref, ra_ref, rb_ref, taps_ref, shift_ref, land_ref, w_ref, stream_ref, qkv_hbm, out_hbm,
    act_in, edge_in, mixed_ref, sent_ref, act_ref, edge_ref, qkv_ref, wout_ref, perm_ref, sem,
    *, chunk, lat,
):
    rows, cols, width_exp = e_ref.shape
    tokens = rows * cols
    steps = width_exp // chunk
    lat_even, pole = even(lat), at_pole(lat)
    copies = [
        pltpu.make_async_copy(src, dst, sem.at[i])
        for i, (src, dst) in enumerate(((qkv_hbm, qkv_ref), (out_hbm, wout_ref)))
    ]
    for copy in copies:
        copy.start()
    perm_ref[...] = send_matrix(rows, cols)

    def conv(i):
        for k in range(chunk // 128):
            lanes = pl.ds(pl.multiple_of(i * chunk + k * 128, 128), 128)
            ra = ra_ref[:, lanes].astype(F32)
            rb = jnp.where(pole, 0.0, rb_ref[:, lanes].astype(F32))
            top = [jnp.where(lat_even, rb, ra)] + [e_ref[r, :, lanes].astype(F32) for r in (0, 1)]
            bottom = [e_ref[r, :, lanes].astype(F32) for r in (rows - 2, rows - 1)]
            bottom += [jnp.where(lat_even, ra, rb)]
            for x, r in ((top, 0), (bottom, rows - 1)):
                filter_line(
                    x, r, lanes, taps_ref, shift_ref, land_ref, edge_ref, act_ref, rows, cols
                )

    def step(i, carry):
        conv(i)
        return carry

    lax.fori_loop(0, steps, step, 0)
    projected = jnp.dot(act_ref[...], w_ref[...], preferred_element_type=F32)
    mixed = (stream_ref[...].reshape(projected.shape).astype(F32) + projected).astype(BF16)
    mixed_ref[...] = mixed
    normed = normalize(mixed.astype(F32)).astype(BF16)
    sent = jnp.dot(perm_ref[...], normed, preferred_element_type=F32)
    for k in range(tokens // 4):
        sent_ref[k] = sent[4 * k : 4 * k + 4].astype(BF16)
    for copy in copies:
        copy.wait()


def edge_kernel(
    edge_ref, left_ref, right_ref, w_ref, stream_ref, sent_ref, inner_ref, mixed_ref, out_ref,
    *, chunk,
):
    double, width_exp = edge_ref.shape
    rows = double // 2
    projected = 0.0
    for at in range(0, width_exp, chunk):
        lanes = slice(at, at + chunk)
        beyond = [ref[:, lanes].astype(F32) for ref in (left_ref, right_ref)]
        act = gelu(edge_ref[:, lanes] + jnp.concatenate(beyond, axis=0)).astype(BF16)
        projected += jnp.dot(act, w_ref[lanes, :], preferred_element_type=F32)
    cols = stream_ref.shape[1]
    first = jnp.concatenate([stream_ref[r, 0:1].astype(F32) for r in range(rows)], axis=0)
    last = jnp.concatenate([stream_ref[r, cols - 1 : cols].astype(F32) for r in range(rows)], axis=0)
    mixed = (jnp.concatenate([first, last], axis=0) + projected).astype(BF16)
    mixed = mixed.astype(F32)
    normed = normalize(mixed).astype(BF16).astype(F32)
    sub = lax.broadcasted_iota(jnp.int32, (cols, mixed.shape[1]), 0)
    for r in range(rows):
        part = slice(r * cols, (r + 1) * cols)
        inner = inner_ref[part].astype(F32)
        inner = jnp.where(sub == 0, mixed[r : r + 1], inner)
        inner = jnp.where(sub == cols - 1, mixed[rows + r : rows + r + 1], inner)
        mixed_ref[part] = inner.astype(BF16)
    pairs = cols // 2
    strips = rows // 2
    for s in range(strips):
        for side, c2 in ((0, 0), (1, pairs - 1)):
            k = s * pairs + c2
            old = sent_ref[k].astype(F32)
            keep = [old[0:1], old[1:2], old[2:3], old[3:4]]
            for m in range(2):
                at = side * rows + m * strips + s
                keep[2 * m + side] = normed[at : at + 1]
            out_ref[k] = jnp.concatenate(keep, axis=0).astype(BF16)


def attend_kernel(x_ref, w_ref, bias_ref, out_ref, x_buf, qk_buf, v_buf, s_buf, p_buf, t_buf, *, heads):
    tokens = 4 * x_ref.shape[0]
    width = x_ref.shape[2]
    head_dim = width // heads
    for k in range(tokens // 4):
        x_buf[4 * k : 4 * k + 4, :] = x_ref[k].astype(F32)
    x = x_buf[...].astype(BF16)
    scale = np.float32(head_dim**-0.5) * LOG2E
    per = 128 // head_dim
    wide = 256
    row_head = lax.broadcasted_iota(jnp.int32, (128, tokens), 0) // head_dim
    ones = jnp.ones((16, tokens), BF16)

    def packs(g):
        return range(g * wide // 128, (g + 1) * wide // 128)

    def span(p):
        return slice(per * tokens * p, per * tokens * (p + 1))

    def project(g):
        for i, ref, at in ((0, qk_buf, 0), (1, qk_buf, width), (2, v_buf, 0)):
            lanes = slice(wide * g, wide * (g + 1))
            w = w_ref[:, i * width + lanes.start : i * width + lanes.stop]
            ref[:, at + lanes.start : at + lanes.stop] = jnp.dot(
                x, w, preferred_element_type=F32
            ).astype(BF16)

    def score(g):
        for p in packs(g):
            q = jnp.transpose(qk_buf[:, 128 * p : 128 * (p + 1)])
            queries = jnp.concatenate(
                [jnp.where(row_head == j, q, jnp.zeros_like(q)) for j in range(per)], axis=1
            )
            keys = qk_buf[:, width + 128 * p : width + 128 * (p + 1)]
            s_buf[:, span(p)] = jnp.dot(keys, queries, preferred_element_type=F32)

    def weigh(g):
        for h in range(g * wide // head_dim, (g + 1) * wide // head_dim):
            base = bias_ref[h]
            bias = jnp.concatenate(
                [base if n == 0 else pltpu.roll(base, 2 * GRID * n, 1) for n in range(GRID)], axis=0
            )
            lanes = slice(tokens * h, tokens * (h + 1))
            s = s_buf[:, lanes] * scale + bias
            p_buf[:, lanes] = jnp.exp2(s - jnp.max(s, axis=0, keepdims=True)).astype(BF16)

    def gather(g):
        for p in packs(g):
            values = jnp.concatenate(
                [jnp.transpose(v_buf[:, 128 * p : 128 * (p + 1)]), ones], axis=0
            )
            summed = jnp.dot(values, p_buf[:, span(p)], preferred_element_type=F32)
            for j in range(per):
                block = summed[:, tokens * j : tokens * (j + 1)]
                at = 128 * p + head_dim * j
                t_buf[at : at + head_dim, :] = block[head_dim * j : head_dim * (j + 1)] * (
                    1.0 / block[128:129]
                )

    def turn(g):
        for p in packs(g):
            x_buf[:, 128 * p : 128 * (p + 1)] = jnp.transpose(t_buf[128 * p : 128 * (p + 1), :])

    for stage, g in (
        (project, 0), (project, 1), (score, 0), (project, 2), (score, 1), (weigh, 0), (score, 2),
        (weigh, 1), (gather, 0), (weigh, 2), (gather, 1), (turn, 0), (gather, 2), (turn, 1), (turn, 2),
    ):
        stage(g)
    for k in range(tokens // 4):
        out_ref[k] = x_buf[4 * k : 4 * k + 4, :].astype(BF16)


def out_kernel(a_ref, w_ref, mixed_ref, out_ref, a_buf, *, rows, cols):
    strips, pairs = rows // 2, cols // 2
    for k in range(a_ref.shape[0]):
        got = a_ref[k].astype(F32)
        for m in range(2):
            at = (m * strips + k // pairs) * cols + 2 * (k % pairs)
            a_buf[at : at + 2, :] = got[2 * m : 2 * m + 2]
    result = mixed_ref[...].astype(F32) + jnp.dot(
        a_buf[...].astype(BF16), w_ref[...], preferred_element_type=F32
    )
    out_ref[...] = result.astype(BF16)


def local(expanded, stream, land, polar, land_shift, dw_kernel, w_proj, w_qkv, w_out, rel_bias):
    rows, cols, width_exp = expanded.shape
    width = stream.shape[2]
    heads = rel_bias.shape[0]
    tokens = rows * cols
    lon, lat = ("nhi", "nlo"), "lat"
    lons, lats = lax.axis_size(lon), lax.axis_size(lat)
    everyone = lon + (lat,)
    swap_core = [(i, i ^ 1) for i in range(lats)]
    swap_next = [(i, (i + 1) % lats if i % 2 else (i - 1) % lats) for i in range(lats)]

    def call(kernel, name, ins, in_specs, outs, scratch, limit, **more):
        return pl.pallas_call(
            kernel,
            name=name,
            out_shape=tuple(pltpu.VMEM(shape, dtype) for shape, dtype in outs),
            in_specs=in_specs,
            out_specs=(VM,) * len(outs),
            scratch_shapes=scratch,
            compiler_params=pltpu.CompilerParams(vmem_limit_bytes=limit << 20),
            **more,
        )(*ins)

    row_shape, col_shape = ((cols, width_exp), BF16), ((rows, width_exp), BF16)
    end_shape = ((2, width_exp), BF16)
    small = (expanded, dw_kernel, land_shift[None], land)
    e_here, taps, shift, land, *picked = call(
        functools.partial(pick_kernel, lat=lat), "pick", map(in_hbm, small), [HBM] * 4,
        [(x.shape, x.dtype) for x in small] + [end_shape] * 2 + [row_shape] * 2 + [col_shape] * 2,
        [pltpu.SemaphoreType.DMA((4,))], 8,
    )
    rel = jnp.transpose(rel_bias, (1, 2, 0)).reshape(-1, heads)
    chunk = 256
    fixed = (e_here, taps, shift, land, *map(in_hbm, (w_proj, rel, polar, stream)))
    inner_outs = [
        ((tokens, width_exp), BF16), ((2 * rows, width_exp), F32), ((tokens, 128), F32),
        (w_proj.shape, BF16), ((heads, 2 * GRID, 128), F32), (stream.shape, BF16),
    ]
    inner_scratch = [
        pltpu.VMEM(rel.shape, F32), pltpu.SMEM(polar.shape, jnp.int32), pltpu.SemaphoreType.DMA((4,)),
    ]
    end_a, end_b, row_a, row_b, first, last = picked
    far_a = lax.ppermute(end_a, lat, swap_core)
    far_b = lax.ppermute(end_b, lat, swap_next)
    got_a = lax.ppermute(row_a, lat, swap_core)
    got_b = lax.ppermute(row_b, lat, swap_next)
    *inner, far_a = call(
        functools.partial(inner_kernel, aliased=1, early=True, chunk=chunk), "inner_early",
        (*fixed, far_a), [VM] * 4 + [HBM] * 4 + [VM],
        inner_outs + [end_shape], inner_scratch, 8, input_output_aliases={8: 6},
    )
    packed = []
    for column, is_last in ((last, True), (first, False)):
        packed += call(
            functools.partial(pack_kernel, lat=lat, is_last=is_last), "pack",
            (column, far_a, far_b, taps, *packed), [VM] * (4 + len(packed)), [col_shape], [], 4,
        )
    from_left = lax.ppermute(packed[0], lon, [(i, (i + 1) % lons) for i in range(lons)])
    from_right = lax.ppermute(packed[1], lon, [(i, (i - 1) % lons) for i in range(lons)])
    act, edge, land_lanes, w_proj, bias, stream = call(
        functools.partial(inner_kernel, aliased=7, early=False, chunk=chunk), "inner_late",
        (*fixed, *inner, packed[0]), [VM] * 4 + [HBM] * 4 + [VM] * 7, inner_outs, inner_scratch, 8,
        input_output_aliases={8 + i: i for i in range(6)},
        cost_estimate=pl.CostEstimate(flops=10**9, bytes_accessed=10**6, transcendentals=0),
    )
    token_shape, sent_shape = ((tokens, width), BF16), ((tokens // 4, 4, width), BF16)
    mixed, sent, act, edge, w_qkv, w_out = call(
        functools.partial(mix_kernel, chunk=chunk, lat=lat), "mix",
        (
            e_here, got_a, got_b, taps, shift, land_lanes, w_proj, stream,
            in_hbm(w_qkv), in_hbm(w_out), act, edge,
        ),
        [VM] * 8 + [HBM] * 2 + [VM] * 2,
        [token_shape, sent_shape] + inner_outs[:2] + [(w_qkv.shape, BF16), (w_out.shape, BF16)],
        [
            pltpu.VMEM((tokens, tokens), BF16), pltpu.SemaphoreType.DMA((2,)),
        ],
        8, input_output_aliases={10: 2, 11: 3},
        cost_estimate=pl.CostEstimate(flops=10**9, bytes_accessed=10**6, transcendentals=0),
    )
    mixed, sent = call(
        functools.partial(edge_kernel, chunk=width), "edge",
        (edge, from_left, from_right, w_proj, stream, sent, mixed), [VM] * 7,
        [token_shape, sent_shape], [], 8, input_output_aliases={5: 1, 6: 0},
    )

    group = ("nhi", lat)
    mine = lax.all_to_all(sent, group, 0, 0, tiled=True)
    attended = pl.pallas_call(
        functools.partial(attend_kernel, heads=heads),
        name="attend",
        out_shape=jax.ShapeDtypeStruct((tokens // 4, 4, width), BF16),
        in_specs=[VM] * 3,
        out_specs=VM,
        scratch_shapes=[
            pltpu.VMEM((tokens, width), F32), pltpu.VMEM((tokens, 2 * width), BF16),
            pltpu.VMEM((tokens, width), BF16), pltpu.VMEM((tokens, tokens * heads), F32),
            pltpu.VMEM((tokens, tokens * heads), BF16), pltpu.VMEM((width, tokens), F32),
        ],
        compiler_params=pltpu.CompilerParams(vmem_limit_bytes=8 << 20),
    )(mine, w_qkv, bias)
    back = lax.all_to_all(attended, group, 0, 0, tiled=True)
    result = pl.pallas_call(
        functools.partial(out_kernel, rows=rows, cols=cols),
        name="out",
        out_shape=jax.ShapeDtypeStruct((tokens, width), BF16),
        in_specs=[VM] * 3,
        out_specs=VM,
        scratch_shapes=[pltpu.VMEM((tokens, width), F32)],
        compiler_params=pltpu.CompilerParams(vmem_limit_bytes=8 << 20),
    )(back, w_out, mixed)
    return result.reshape(rows, cols, width)


def solution(mesh):
    lons, lats = mesh.shape["lon"], mesh.shape["lat"]
    fine = Mesh(mesh.devices.reshape(GRID, lons // GRID, lats), ("nhi", "nlo", "lat"))
    lon = ("nhi", "nlo")
    in_specs = (P("lat", lon, None), P("lat", lon, None), P("lat", lon)) + (P(),) * 7
    return jax.shard_map(
        local, mesh=fine, in_specs=in_specs, out_specs=P("lat", lon, None), check_vma=False
    )
```

```python
import functools

import jax
import jax.numpy as jnp
import numpy as np
from jax import lax
from jax.experimental import pallas as pl
from jax.experimental.pallas import tpu as pltpu
from jax.sharding import Mesh
from jax.sharding import PartitionSpec as P

GRID = 8
EPS = 1e-05
NEG = -1e30
LOG2E = np.float32(np.log2(np.e))
F32 = jnp.float32
BF16 = jnp.bfloat16
VM = pl.BlockSpec(memory_space=pltpu.VMEM)
SM = pl.BlockSpec(memory_space=pltpu.SMEM)
HBM = pl.BlockSpec(memory_space=pltpu.HBM)


def at_pole(lat):
    at = lax.axis_index(lat)
    return (at == 0) | (at == lax.axis_size(lat) - 1)


def in_hbm(x):
    return pltpu.with_memory_space_constraint(x, pltpu.HBM)


def send_matrix(rows, cols):
    tokens = rows * cols
    strips, pairs = rows // 2, cols // 2
    to = lax.broadcasted_iota(jnp.int32, (tokens, tokens), 0)
    at = lax.broadcasted_iota(jnp.int32, (tokens, tokens), 1)
    s, rest = to // (4 * pairs), to % (4 * pairs)
    c2, m, c1 = rest // 4, rest % 4 // 2, rest % 2
    token = (m * strips + s) * cols + 2 * c2 + c1
    return jnp.where(token == at, 1.0, 0.0).astype(BF16)


def even(axes):
    return lax.rem(lax.axis_index(axes), 2) == 0


def pick_kernel(*refs, lat):
    ins, outs, (xa_ref, xb_ref, ra_ref, rb_ref, first, last, sem) = refs[:4], refs[4:8], refs[8:]
    e_ref = outs[0]
    rows, cols, _ = e_ref.shape
    copies = [
        pltpu.make_async_copy(src, dst, sem.at[i]) for i, (src, dst) in enumerate(zip(ins, outs))
    ]
    for copy in copies:
        copy.start()
    lat_even = even(lat)
    copies[0].wait()
    ra_ref[...] = jnp.where(lat_even, e_ref[rows - 1], e_ref[0])
    rb_ref[...] = jnp.where(lat_even, e_ref[0], e_ref[rows - 1])
    lines = [e_ref[r].astype(F32) for r in range(rows)]
    a = jnp.concatenate([line[0:1] for line in lines], axis=0)
    b = jnp.concatenate([line[cols - 1 : cols] for line in lines], axis=0)
    first[...] = a.astype(BF16)
    last[...] = b.astype(BF16)
    above = jnp.concatenate([a[0:1], b[0:1]], axis=0)
    below = jnp.concatenate([a[rows - 1 : rows], b[rows - 1 : rows]], axis=0)
    xa_ref[...] = jnp.where(lat_even, below, above).astype(BF16)
    xb_ref[...] = jnp.where(lat_even, above, below).astype(BF16)
    for copy in copies[1:]:
        copy.wait()


def pack_kernel(c_ref, xa_ref, xb_ref, taps_ref, o_ref, *, lat, is_last):
    lat_even = even(lat)
    rows = c_ref.shape[0]
    end, tap = (1, 0) if is_last else (0, 2)
    xa, xb = (ref[end : end + 1].astype(F32) for ref in (xa_ref, xb_ref))
    xb = jnp.where(at_pole(lat), 0.0, xb)
    above, below = jnp.where(lat_even, xb, xa), jnp.where(lat_even, xa, xb)
    sub = lax.broadcasted_iota(jnp.int32, c_ref.shape, 0)
    here = c_ref[...].astype(F32)
    above = jnp.where(sub == 0, above, pltpu.roll(here, 1, 0))
    below = jnp.where(sub == rows - 1, below, pltpu.roll(here, rows - 1, 0))
    tap = [taps_ref[i, tap : tap + 1] for i in range(3)]
    o_ref[...] = (tap[0] * above + tap[1] * here + tap[2] * below).astype(BF16)


def gelu(x):
    inner = x * (np.float32(np.sqrt(2 / np.pi)) + np.float32(0.044715 * np.sqrt(2 / np.pi)) * (x * x))
    half = np.float32(0.5) * x
    return half + half * jnp.tanh(inner)


def normalize(flat):
    centred = flat - jnp.mean(flat, axis=1, keepdims=True)
    spread = jnp.mean(centred * centred, axis=1, keepdims=True)
    return centred * lax.rsqrt(spread + EPS)


def fill_bias(polar, rel, out_ref, strips, nhi):
    strip = lax.axis_index(nhi) * strips // lax.axis_size(nhi)
    high = rel.astype(BF16)
    middle = (rel - high.astype(F32)).astype(BF16)
    low = (rel - high.astype(F32) - middle.astype(F32)).astype(BF16)
    offsets = rel.shape[0]
    lane = lax.broadcasted_iota(jnp.int32, (offsets, 128), 1)
    mq = lane // 2 % GRID
    nq = lane // (2 * GRID)
    at = lax.broadcasted_iota(jnp.int32, (offsets, 128), 0)
    gq = lax.broadcasted_iota(jnp.int32, (1, 128), 1) % 2
    for mk in range(GRID):
        wanted = (mk - mq + GRID - 1) * GRID + (GRID - nq) % GRID
        choose = jnp.where(at == wanted, 1.0, 0.0).astype(BF16)
        near = sum(
            lax.dot_general(
                part, choose, (((0,), (0,)), ((), ())), preferred_element_type=F32
            )
            for part in (high, middle, low)
        )
        cap = jnp.where(polar[mk * strips + strip] == 1, np.float32(NEG), np.float32(0.0))
        for gk in range(2):
            out_ref[:, 2 * mk + gk, :] = near * LOG2E + jnp.where(gq == gk, cap, np.float32(NEG))


def filter_line(x, r, lanes, taps_ref, shift_ref, land_ref, edge_ref, act_ref, rows, cols):
    sub = lax.broadcasted_iota(jnp.int32, (cols, 128), 0)
    tap = [[taps_ref[a, b : b + 1, lanes] for b in range(3)] for a in range(3)]
    y = [tap[0][b] * x[0] + tap[1][b] * x[1] + tap[2][b] * x[2] for b in range(3)]
    y0 = jnp.where(sub == 0, 0.0, pltpu.roll(y[0], 1, 0))
    y2 = jnp.where(sub == cols - 1, 0.0, pltpu.roll(y[2], cols - 1, 0))
    filtered = land_ref[r * cols : (r + 1) * cols] * shift_ref[:, lanes] + y[1] + (y0 + y2)
    edge_ref[r : r + 1, lanes] = filtered[0:1]
    edge_ref[rows + r : rows + r + 1, lanes] = filtered[cols - 1 : cols]
    act_ref[r * cols : (r + 1) * cols, lanes] = gelu(filtered).astype(BF16)


def spread_land(land, cols):
    rows = land.shape[0]
    tokens = rows * cols
    token = lax.broadcasted_iota(jnp.int32, (tokens, cols), 0)
    at = lax.broadcasted_iota(jnp.int32, (tokens, cols), 1)
    row_of = lax.broadcasted_iota(jnp.int32, (tokens, rows), 0) // cols
    pick_row = (row_of == lax.broadcasted_iota(jnp.int32, (tokens, rows), 1)).astype(F32)
    by_row = jnp.dot(pick_row, land.astype(F32), preferred_element_type=F32)
    mine = jnp.where(lax.rem(token, cols) == at, by_row, 0.0)
    return jnp.dot(mine, jnp.ones((cols, 128), F32), preferred_element_type=F32)


def inner_kernel(*refs, aliased, early, chunk):
    ins, refs = refs[:8], refs[8 + aliased :]
    outs, (rel_ref, polar_ref, sem) = refs[:-3], refs[-3:]
    e_ref, taps_ref, shift_ref, land_raw, w_hbm, rel_hbm, polar_hbm, stream_hbm = ins
    act_ref, edge_ref, land_ref, w_ref, bias_ref, stream_ref = outs[:6]
    rows, cols, width_exp = e_ref.shape
    here = lax.axis_index("nlo") == 0

    @pl.when(here if early else ~here)
    def _():
        copies = [
            pltpu.make_async_copy(src, dst, sem.at[i])
            for i, (src, dst) in enumerate(
                (
                    (rel_hbm, rel_ref), (polar_hbm, polar_ref), (w_hbm, w_ref),
                    (stream_hbm, stream_ref),
                )
            )
        ]
        for copy in copies:
            copy.start()
        land_ref[...] = spread_land(land_raw[...], cols)

        def step(i, carry):
            lanes = pl.ds(pl.multiple_of(i * 128, 128), 128)
            x = [e_ref[r, :, lanes].astype(F32) for r in range(rows)]
            for r in range(1, rows - 1):
                filter_line(
                    x[r - 1 : r + 2], r, lanes, taps_ref, shift_ref, land_ref, edge_ref, act_ref,
                    rows, cols,
                )
            return carry

        lax.fori_loop(0, width_exp // 128, step, 0)
        for copy in copies[:2]:
            copy.wait()
        fill_bias(polar_ref, rel_ref[...], bias_ref, rows // 2, "nhi")
        for copy in copies[2:]:
            copy.wait()


def mix_kernel(
    e_ref, ra_ref, rb_ref, taps_ref, shift_ref, land_ref, w_ref, stream_ref, qkv_hbm, out_hbm,
    act_in, edge_in, mixed_ref, sent_ref, act_ref, edge_ref, qkv_ref, wout_ref, perm_ref, sem,
    *, chunk, lat,
):
    rows, cols, width_exp = e_ref.shape
    tokens = rows * cols
    steps = width_exp // chunk
    lat_even, pole = even(lat), at_pole(lat)
    copies = [
        pltpu.make_async_copy(src, dst, sem.at[i])
        for i, (src, dst) in enumerate(((qkv_hbm, qkv_ref), (out_hbm, wout_ref)))
    ]
    for copy in copies:
        copy.start()
    perm_ref[...] = send_matrix(rows, cols)

    def conv(i):
        for k in range(chunk // 128):
            lanes = pl.ds(pl.multiple_of(i * chunk + k * 128, 128), 128)
            ra = ra_ref[:, lanes].astype(F32)
            rb = jnp.where(pole, 0.0, rb_ref[:, lanes].astype(F32))
            top = [jnp.where(lat_even, rb, ra)] + [e_ref[r, :, lanes].astype(F32) for r in (0, 1)]
            bottom = [e_ref[r, :, lanes].astype(F32) for r in (rows - 2, rows - 1)]
            bottom += [jnp.where(lat_even, ra, rb)]
            for x, r in ((top, 0), (bottom, rows - 1)):
                filter_line(
                    x, r, lanes, taps_ref, shift_ref, land_ref, edge_ref, act_ref, rows, cols
                )

    def step(i, carry):
        conv(i)
        return carry

    lax.fori_loop(0, steps, step, 0)
    projected = jnp.dot(act_ref[...], w_ref[...], preferred_element_type=F32)
    mixed = (stream_ref[...].reshape(projected.shape).astype(F32) + projected).astype(BF16)
    mixed_ref[...] = mixed
    normed = normalize(mixed.astype(F32)).astype(BF16)
    sent = jnp.dot(perm_ref[...], normed, preferred_element_type=F32)
    for k in range(tokens // 4):
        sent_ref[k] = sent[4 * k : 4 * k + 4].astype(BF16)
    for copy in copies:
        copy.wait()


def edge_kernel(
    edge_ref, left_ref, right_ref, w_ref, stream_ref, sent_ref, inner_ref, mixed_ref, out_ref,
    *, chunk,
):
    double, width_exp = edge_ref.shape
    rows = double // 2
    projected = 0.0
    for at in range(0, width_exp, chunk):
        lanes = slice(at, at + chunk)
        beyond = [ref[:, lanes].astype(F32) for ref in (left_ref, right_ref)]
        act = gelu(edge_ref[:, lanes] + jnp.concatenate(beyond, axis=0)).astype(BF16)
        projected += jnp.dot(act, w_ref[lanes, :], preferred_element_type=F32)
    cols = stream_ref.shape[1]
    first = jnp.concatenate([stream_ref[r, 0:1].astype(F32) for r in range(rows)], axis=0)
    last = jnp.concatenate([stream_ref[r, cols - 1 : cols].astype(F32) for r in range(rows)], axis=0)
    mixed = (jnp.concatenate([first, last], axis=0) + projected).astype(BF16)
    mixed = mixed.astype(F32)
    normed = normalize(mixed).astype(BF16).astype(F32)
    sub = lax.broadcasted_iota(jnp.int32, (cols, mixed.shape[1]), 0)
    for r in range(rows):
        part = slice(r * cols, (r + 1) * cols)
        inner = inner_ref[part].astype(F32)
        inner = jnp.where(sub == 0, mixed[r : r + 1], inner)
        inner = jnp.where(sub == cols - 1, mixed[rows + r : rows + r + 1], inner)
        mixed_ref[part] = inner.astype(BF16)
    pairs = cols // 2
    strips = rows // 2
    for s in range(strips):
        for side, c2 in ((0, 0), (1, pairs - 1)):
            k = s * pairs + c2
            old = sent_ref[k].astype(F32)
            keep = [old[0:1], old[1:2], old[2:3], old[3:4]]
            for m in range(2):
                at = side * rows + m * strips + s
                keep[2 * m + side] = normed[at : at + 1]
            out_ref[k] = jnp.concatenate(keep, axis=0).astype(BF16)


def attend_kernel(x_ref, w_ref, bias_ref, out_ref, x_buf, qk_buf, v_buf, s_buf, p_buf, t_buf, *, heads):
    tokens = 4 * x_ref.shape[0]
    width = x_ref.shape[2]
    head_dim = width // heads
    for k in range(tokens // 4):
        x_buf[4 * k : 4 * k + 4, :] = x_ref[k].astype(F32)
    x = x_buf[...].astype(BF16)
    scale = np.float32(head_dim**-0.5) * LOG2E
    per = 128 // head_dim
    wide = 256
    row_head = lax.broadcasted_iota(jnp.int32, (128, tokens), 0) // head_dim
    ones = jnp.ones((16, tokens), BF16)

    def packs(g):
        return range(g * wide // 128, (g + 1) * wide // 128)

    def span(p):
        return slice(per * tokens * p, per * tokens * (p + 1))

    def project(g):
        for i, ref, at in ((0, qk_buf, 0), (1, qk_buf, width), (2, v_buf, 0)):
            lanes = slice(wide * g, wide * (g + 1))
            w = w_ref[:, i * width + lanes.start : i * width + lanes.stop]
            ref[:, at + lanes.start : at + lanes.stop] = jnp.dot(
                x, w, preferred_element_type=F32
            ).astype(BF16)

    def score(g):
        for p in packs(g):
            q = jnp.transpose(qk_buf[:, 128 * p : 128 * (p + 1)])
            queries = jnp.concatenate(
                [jnp.where(row_head == j, q, jnp.zeros_like(q)) for j in range(per)], axis=1
            )
            keys = qk_buf[:, width + 128 * p : width + 128 * (p + 1)]
            s_buf[:, span(p)] = jnp.dot(keys, queries, preferred_element_type=F32)

    def weigh(g):
        for h in range(g * wide // head_dim, (g + 1) * wide // head_dim):
            base = bias_ref[h]
            bias = jnp.concatenate(
                [base if n == 0 else pltpu.roll(base, 2 * GRID * n, 1) for n in range(GRID)], axis=0
            )
            lanes = slice(tokens * h, tokens * (h + 1))
            s = s_buf[:, lanes] * scale + bias
            p_buf[:, lanes] = jnp.exp2(s - jnp.max(s, axis=0, keepdims=True)).astype(BF16)

    def gather(g):
        for p in packs(g):
            values = jnp.concatenate(
                [jnp.transpose(v_buf[:, 128 * p : 128 * (p + 1)]), ones], axis=0
            )
            summed = jnp.dot(values, p_buf[:, span(p)], preferred_element_type=F32)
            for j in range(per):
                block = summed[:, tokens * j : tokens * (j + 1)]
                at = 128 * p + head_dim * j
                t_buf[at : at + head_dim, :] = block[head_dim * j : head_dim * (j + 1)] * (
                    1.0 / block[128:129]
                )

    def turn(g):
        for p in packs(g):
            x_buf[:, 128 * p : 128 * (p + 1)] = jnp.transpose(t_buf[128 * p : 128 * (p + 1), :])

    for stage, g in (
        (project, 0), (project, 1), (score, 0), (project, 2), (score, 1), (weigh, 0), (score, 2),
        (weigh, 1), (gather, 0), (weigh, 2), (gather, 1), (turn, 0), (gather, 2), (turn, 1), (turn, 2),
    ):
        stage(g)
    for k in range(tokens // 4):
        out_ref[k] = x_buf[4 * k : 4 * k + 4, :].astype(BF16)


def out_kernel(a_ref, w_ref, mixed_ref, out_ref, a_buf, *, rows, cols):
    strips, pairs = rows // 2, cols // 2
    for k in range(a_ref.shape[0]):
        got = a_ref[k].astype(F32)
        for m in range(2):
            at = (m * strips + k // pairs) * cols + 2 * (k % pairs)
            a_buf[at : at + 2, :] = got[2 * m : 2 * m + 2]
    result = mixed_ref[...].astype(F32) + jnp.dot(
        a_buf[...].astype(BF16), w_ref[...], preferred_element_type=F32
    )
    out_ref[...] = result.astype(BF16)


def local(expanded, stream, land, polar, land_shift, dw_kernel, w_proj, w_qkv, w_out, rel_bias):
    rows, cols, width_exp = expanded.shape
    width = stream.shape[2]
    heads = rel_bias.shape[0]
    tokens = rows * cols
    lon, lat = ("nhi", "nlo"), "lat"
    lons, lats = lax.axis_size(lon), lax.axis_size(lat)
    everyone = lon + (lat,)
    swap_core = [(i, i ^ 1) for i in range(lats)]
    swap_next = [(i, (i + 1) % lats if i % 2 else (i - 1) % lats) for i in range(lats)]

    def call(kernel, name, ins, in_specs, outs, scratch, limit, **more):
        return pl.pallas_call(
            kernel,
            name=name,
            out_shape=tuple(pltpu.VMEM(shape, dtype) for shape, dtype in outs),
            in_specs=in_specs,
            out_specs=(VM,) * len(outs),
            scratch_shapes=scratch,
            compiler_params=pltpu.CompilerParams(vmem_limit_bytes=limit << 20),
            **more,
        )(*ins)

    row_shape, col_shape = ((cols, width_exp), BF16), ((rows, width_exp), BF16)
    end_shape = ((2, width_exp), BF16)
    small = (expanded, dw_kernel, land_shift[None], land)
    e_here, taps, shift, land, *picked = call(
        functools.partial(pick_kernel, lat=lat), "pick", map(in_hbm, small), [HBM] * 4,
        [(x.shape, x.dtype) for x in small] + [end_shape] * 2 + [row_shape] * 2 + [col_shape] * 2,
        [pltpu.SemaphoreType.DMA((4,))], 8,
    )
    rel = jnp.transpose(rel_bias, (1, 2, 0)).reshape(-1, heads)
    chunk = 256
    fixed = (e_here, taps, shift, land, *map(in_hbm, (w_proj, rel, polar, stream)))
    inner_outs = [
        ((tokens, width_exp), BF16), ((2 * rows, width_exp), F32), ((tokens, 128), F32),
        (w_proj.shape, BF16), ((heads, 2 * GRID, 128), F32), (stream.shape, BF16),
    ]
    inner_scratch = [
        pltpu.VMEM(rel.shape, F32), pltpu.SMEM(polar.shape, jnp.int32), pltpu.SemaphoreType.DMA((4,)),
    ]
    end_a, end_b, row_a, row_b, first, last = picked
    far_a = lax.ppermute(end_a, lat, swap_core)
    far_b = lax.ppermute(end_b, lat, swap_next)
    got_a = lax.ppermute(row_a, lat, swap_core)
    got_b = lax.ppermute(row_b, lat, swap_next)

    def pack(column, is_last):
        return call(
            functools.partial(pack_kernel, lat=lat, is_last=is_last), "pack",
            (column, far_a, far_b, taps), [VM] * 4, [col_shape], [], 4,
        )[0]

    rightward = pack(last, True)
    from_left = lax.ppermute(rightward, lon, [(i, (i + 1) % lons) for i in range(lons)])
    *inner, first = call(
        functools.partial(inner_kernel, aliased=2, early=True, chunk=chunk), "inner_early",
        (*fixed, first, rightward), [VM] * 4 + [HBM] * 4 + [VM] * 2,
        inner_outs + [col_shape], inner_scratch, 8, input_output_aliases={8: 6},
    )
    leftward = pack(first, False)
    from_right = lax.ppermute(leftward, lon, [(i, (i - 1) % lons) for i in range(lons)])
    act, edge, land_lanes, w_proj, bias, stream = call(
        functools.partial(inner_kernel, aliased=7, early=False, chunk=chunk), "inner_late",
        (*fixed, *inner, leftward), [VM] * 4 + [HBM] * 4 + [VM] * 7, inner_outs, inner_scratch, 8,
        input_output_aliases={8 + i: i for i in range(6)},
        cost_estimate=pl.CostEstimate(flops=10**9, bytes_accessed=10**6, transcendentals=0),
    )
    token_shape, sent_shape = ((tokens, width), BF16), ((tokens // 4, 4, width), BF16)
    mixed, sent, act, edge, w_qkv, w_out = call(
        functools.partial(mix_kernel, chunk=chunk, lat=lat), "mix",
        (
            e_here, got_a, got_b, taps, shift, land_lanes, w_proj, stream,
            in_hbm(w_qkv), in_hbm(w_out), act, edge,
        ),
        [VM] * 8 + [HBM] * 2 + [VM] * 2,
        [token_shape, sent_shape] + inner_outs[:2] + [(w_qkv.shape, BF16), (w_out.shape, BF16)],
        [
            pltpu.VMEM((tokens, tokens), BF16), pltpu.SemaphoreType.DMA((2,)),
        ],
        8, input_output_aliases={10: 2, 11: 3},
        cost_estimate=pl.CostEstimate(flops=10**9, bytes_accessed=10**6, transcendentals=0),
    )
    mixed, sent = call(
        functools.partial(edge_kernel, chunk=width), "edge",
        (edge, from_left, from_right, w_proj, stream, sent, mixed), [VM] * 7,
        [token_shape, sent_shape], [], 8, input_output_aliases={5: 1, 6: 0},
    )

    group = ("nhi", lat)
    mine = lax.all_to_all(sent, group, 0, 0, tiled=True)
    attended = pl.pallas_call(
        functools.partial(attend_kernel, heads=heads),
        name="attend",
        out_shape=jax.ShapeDtypeStruct((tokens // 4, 4, width), BF16),
        in_specs=[VM] * 3,
        out_specs=VM,
        scratch_shapes=[
            pltpu.VMEM((tokens, width), F32), pltpu.VMEM((tokens, 2 * width), BF16),
            pltpu.VMEM((tokens, width), BF16), pltpu.VMEM((tokens, tokens * heads), F32),
            pltpu.VMEM((tokens, tokens * heads), BF16), pltpu.VMEM((width, tokens), F32),
        ],
        compiler_params=pltpu.CompilerParams(vmem_limit_bytes=8 << 20),
    )(mine, w_qkv, bias)
    back = lax.all_to_all(attended, group, 0, 0, tiled=True)
    result = pl.pallas_call(
        functools.partial(out_kernel, rows=rows, cols=cols),
        name="out",
        out_shape=jax.ShapeDtypeStruct((tokens, width), BF16),
        in_specs=[VM] * 3,
        out_specs=VM,
        scratch_shapes=[pltpu.VMEM((tokens, width), F32)],
        compiler_params=pltpu.CompilerParams(vmem_limit_bytes=8 << 20),
    )(back, w_out, mixed)
    return result.reshape(rows, cols, width)


def solution(mesh):
    lons, lats = mesh.shape["lon"], mesh.shape["lat"]
    fine = Mesh(mesh.devices.reshape(GRID, lons // GRID, lats), ("nhi", "nlo", "lat"))
    lon = ("nhi", "nlo")
    in_specs = (P("lat", lon, None), P("lat", lon, None), P("lat", lon)) + (P(),) * 7
    return jax.shard_map(
        local, mesh=fine, in_specs=in_specs, out_specs=P("lat", lon, None), check_vma=False
    )
```

```python
import functools

import jax
import jax.numpy as jnp
import numpy as np
from jax import lax
from jax.experimental import pallas as pl
from jax.experimental.pallas import tpu as pltpu
from jax.sharding import Mesh
from jax.sharding import PartitionSpec as P

GRID = 8
EPS = 1e-05
NEG = -1e30
LOG2E = np.float32(np.log2(np.e))
F32 = jnp.float32
BF16 = jnp.bfloat16
VM = pl.BlockSpec(memory_space=pltpu.VMEM)
SM = pl.BlockSpec(memory_space=pltpu.SMEM)
HBM = pl.BlockSpec(memory_space=pltpu.HBM)


def at_pole(lat):
    at = lax.axis_index(lat)
    return (at == 0) | (at == lax.axis_size(lat) - 1)


def in_hbm(x):
    return pltpu.with_memory_space_constraint(x, pltpu.HBM)


def send_matrix(rows, cols):
    tokens = rows * cols
    strips, pairs = rows // 2, cols // 2
    to = lax.broadcasted_iota(jnp.int32, (tokens, tokens), 0)
    at = lax.broadcasted_iota(jnp.int32, (tokens, tokens), 1)
    s, rest = to // (4 * pairs), to % (4 * pairs)
    c2, m, c1 = rest // 4, rest % 4 // 2, rest % 2
    token = (m * strips + s) * cols + 2 * c2 + c1
    return jnp.where(token == at, 1.0, 0.0).astype(BF16)


def even(axes):
    return lax.rem(lax.axis_index(axes), 2) == 0


def pick_kernel(*refs, lat):
    ins, outs, (xa_ref, xb_ref, ra_ref, rb_ref, first, last, sem) = refs[:4], refs[4:8], refs[8:]
    e_ref = outs[0]
    rows, cols, _ = e_ref.shape
    copies = [
        pltpu.make_async_copy(src, dst, sem.at[i]) for i, (src, dst) in enumerate(zip(ins, outs))
    ]
    for copy in copies:
        copy.start()
    lat_even = even(lat)
    copies[0].wait()
    ra_ref[...] = jnp.where(lat_even, e_ref[rows - 1], e_ref[0])
    rb_ref[...] = jnp.where(lat_even, e_ref[0], e_ref[rows - 1])
    lines = [e_ref[r].astype(F32) for r in range(rows)]
    a = jnp.concatenate([line[0:1] for line in lines], axis=0)
    b = jnp.concatenate([line[cols - 1 : cols] for line in lines], axis=0)
    first[...] = a.astype(BF16)
    last[...] = b.astype(BF16)
    above = jnp.concatenate([a[0:1], b[0:1]], axis=0)
    below = jnp.concatenate([a[rows - 1 : rows], b[rows - 1 : rows]], axis=0)
    xa_ref[...] = jnp.where(lat_even, below, above).astype(BF16)
    xb_ref[...] = jnp.where(lat_even, above, below).astype(BF16)
    for copy in copies[1:]:
        copy.wait()


def pack_kernel(c_ref, xa_ref, xb_ref, taps_ref, o_ref, *, lat, is_last):
    lat_even = even(lat)
    rows = c_ref.shape[0]
    end, tap = (1, 0) if is_last else (0, 2)
    xa, xb = (ref[end : end + 1].astype(F32) for ref in (xa_ref, xb_ref))
    xb = jnp.where(at_pole(lat), 0.0, xb)
    above, below = jnp.where(lat_even, xb, xa), jnp.where(lat_even, xa, xb)
    sub = lax.broadcasted_iota(jnp.int32, c_ref.shape, 0)
    here = c_ref[...].astype(F32)
    above = jnp.where(sub == 0, above, pltpu.roll(here, 1, 0))
    below = jnp.where(sub == rows - 1, below, pltpu.roll(here, rows - 1, 0))
    tap = [taps_ref[i, tap : tap + 1] for i in range(3)]
    o_ref[...] = (tap[0] * above + tap[1] * here + tap[2] * below).astype(BF16)


def gelu(x):
    inner = x * (np.float32(np.sqrt(2 / np.pi)) + np.float32(0.044715 * np.sqrt(2 / np.pi)) * (x * x))
    half = np.float32(0.5) * x
    return half + half * jnp.tanh(inner)


def normalize(flat):
    centred = flat - jnp.mean(flat, axis=1, keepdims=True)
    spread = jnp.mean(centred * centred, axis=1, keepdims=True)
    return centred * lax.rsqrt(spread + EPS)


def fill_bias(polar, rel, out_ref, strips, nhi):
    strip = lax.axis_index(nhi) * strips // lax.axis_size(nhi)
    high = rel.astype(BF16)
    middle = (rel - high.astype(F32)).astype(BF16)
    low = (rel - high.astype(F32) - middle.astype(F32)).astype(BF16)
    offsets = rel.shape[0]
    lane = lax.broadcasted_iota(jnp.int32, (offsets, 128), 1)
    mq = lane // 2 % GRID
    nq = lane // (2 * GRID)
    at = lax.broadcasted_iota(jnp.int32, (offsets, 128), 0)
    gq = lax.broadcasted_iota(jnp.int32, (1, 128), 1) % 2
    for mk in range(GRID):
        wanted = (mk - mq + GRID - 1) * GRID + (GRID - nq) % GRID
        choose = jnp.where(at == wanted, 1.0, 0.0).astype(BF16)
        near = sum(
            lax.dot_general(
                part, choose, (((0,), (0,)), ((), ())), preferred_element_type=F32
            )
            for part in (high, middle, low)
        )
        cap = jnp.where(polar[mk * strips + strip] == 1, np.float32(NEG), np.float32(0.0))
        for gk in range(2):
            out_ref[:, 2 * mk + gk, :] = near * LOG2E + jnp.where(gq == gk, cap, np.float32(NEG))


def filter_line(x, r, lanes, taps_ref, shift_ref, land_ref, edge_ref, act_ref, rows, cols):
    sub = lax.broadcasted_iota(jnp.int32, (cols, 128), 0)
    tap = [[taps_ref[a, b : b + 1, lanes] for b in range(3)] for a in range(3)]
    y = [tap[0][b] * x[0] + tap[1][b] * x[1] + tap[2][b] * x[2] for b in range(3)]
    y0 = jnp.where(sub == 0, 0.0, pltpu.roll(y[0], 1, 0))
    y2 = jnp.where(sub == cols - 1, 0.0, pltpu.roll(y[2], cols - 1, 0))
    filtered = land_ref[r * cols : (r + 1) * cols] * shift_ref[:, lanes] + y[1] + (y0 + y2)
    edge_ref[r : r + 1, lanes] = filtered[0:1]
    edge_ref[rows + r : rows + r + 1, lanes] = filtered[cols - 1 : cols]
    act_ref[r * cols : (r + 1) * cols, lanes] = gelu(filtered).astype(BF16)


def spread_land(land, cols):
    rows = land.shape[0]
    tokens = rows * cols
    token = lax.broadcasted_iota(jnp.int32, (tokens, cols), 0)
    at = lax.broadcasted_iota(jnp.int32, (tokens, cols), 1)
    row_of = lax.broadcasted_iota(jnp.int32, (tokens, rows), 0) // cols
    pick_row = (row_of == lax.broadcasted_iota(jnp.int32, (tokens, rows), 1)).astype(F32)
    by_row = jnp.dot(pick_row, land.astype(F32), preferred_element_type=F32)
    mine = jnp.where(lax.rem(token, cols) == at, by_row, 0.0)
    return jnp.dot(mine, jnp.ones((cols, 128), F32), preferred_element_type=F32)


def inner_kernel(*refs, aliased, early, chunk):
    ins, refs = refs[:8], refs[8 + aliased :]
    outs, (rel_ref, polar_ref, sem) = refs[:-3], refs[-3:]
    e_ref, taps_ref, shift_ref, land_raw, w_hbm, rel_hbm, polar_hbm, stream_hbm = ins
    act_ref, edge_ref, land_ref, w_ref, bias_ref, stream_ref = outs[:6]
    rows, cols, width_exp = e_ref.shape
    here = lax.axis_index("nlo") == 0

    @pl.when(here if early else ~here)
    def _():
        copies = [
            pltpu.make_async_copy(src, dst, sem.at[i])
            for i, (src, dst) in enumerate(
                (
                    (rel_hbm, rel_ref), (polar_hbm, polar_ref), (w_hbm, w_ref),
                    (stream_hbm, stream_ref),
                )
            )
        ]
        for copy in copies:
            copy.start()
        land_ref[...] = spread_land(land_raw[...], cols)

        def step(i, carry):
            lanes = pl.ds(pl.multiple_of(i * 128, 128), 128)
            x = [e_ref[r, :, lanes].astype(F32) for r in range(rows)]
            for r in range(1, rows - 1):
                filter_line(
                    x[r - 1 : r + 2], r, lanes, taps_ref, shift_ref, land_ref, edge_ref, act_ref,
                    rows, cols,
                )
            return carry

        lax.fori_loop(0, width_exp // 128, step, 0, unroll=2)
        for copy in copies[:2]:
            copy.wait()
        fill_bias(polar_ref, rel_ref[...], bias_ref, rows // 2, "nhi")
        for copy in copies[2:]:
            copy.wait()


def mix_kernel(
    e_ref, ra_ref, rb_ref, taps_ref, shift_ref, land_ref, w_ref, stream_ref, qkv_hbm, out_hbm,
    act_in, edge_in, mixed_ref, sent_ref, act_ref, edge_ref, qkv_ref, wout_ref, perm_ref, sem,
    *, chunk, lat,
):
    rows, cols, width_exp = e_ref.shape
    tokens = rows * cols
    steps = width_exp // chunk
    lat_even, pole = even(lat), at_pole(lat)
    copies = [
        pltpu.make_async_copy(src, dst, sem.at[i])
        for i, (src, dst) in enumerate(((qkv_hbm, qkv_ref), (out_hbm, wout_ref)))
    ]
    for copy in copies:
        copy.start()
    perm_ref[...] = send_matrix(rows, cols)

    def conv(i):
        for k in range(chunk // 128):
            lanes = pl.ds(pl.multiple_of(i * chunk + k * 128, 128), 128)
            ra = ra_ref[:, lanes].astype(F32)
            rb = jnp.where(pole, 0.0, rb_ref[:, lanes].astype(F32))
            top = [jnp.where(lat_even, rb, ra)] + [e_ref[r, :, lanes].astype(F32) for r in (0, 1)]
            bottom = [e_ref[r, :, lanes].astype(F32) for r in (rows - 2, rows - 1)]
            bottom += [jnp.where(lat_even, ra, rb)]
            for x, r in ((top, 0), (bottom, rows - 1)):
                filter_line(
                    x, r, lanes, taps_ref, shift_ref, land_ref, edge_ref, act_ref, rows, cols
                )

    def step(i, carry):
        conv(i)
        return carry

    lax.fori_loop(0, steps, step, 0)
    projected = jnp.dot(act_ref[...], w_ref[...], preferred_element_type=F32)
    mixed = (stream_ref[...].reshape(projected.shape).astype(F32) + projected).astype(BF16)
    mixed_ref[...] = mixed
    normed = normalize(mixed.astype(F32)).astype(BF16)
    sent = jnp.dot(perm_ref[...], normed, preferred_element_type=F32)
    for k in range(tokens // 4):
        sent_ref[k] = sent[4 * k : 4 * k + 4].astype(BF16)
    for copy in copies:
        copy.wait()


def edge_kernel(
    edge_ref, left_ref, right_ref, w_ref, stream_ref, sent_ref, inner_ref, mixed_ref, out_ref,
    *, chunk,
):
    double, width_exp = edge_ref.shape
    rows = double // 2
    projected = 0.0
    for at in range(0, width_exp, chunk):
        lanes = slice(at, at + chunk)
        beyond = [ref[:, lanes].astype(F32) for ref in (left_ref, right_ref)]
        act = gelu(edge_ref[:, lanes] + jnp.concatenate(beyond, axis=0)).astype(BF16)
        projected += jnp.dot(act, w_ref[lanes, :], preferred_element_type=F32)
    cols = stream_ref.shape[1]
    first = jnp.concatenate([stream_ref[r, 0:1].astype(F32) for r in range(rows)], axis=0)
    last = jnp.concatenate([stream_ref[r, cols - 1 : cols].astype(F32) for r in range(rows)], axis=0)
    mixed = (jnp.concatenate([first, last], axis=0) + projected).astype(BF16)
    mixed = mixed.astype(F32)
    normed = normalize(mixed).astype(BF16).astype(F32)
    sub = lax.broadcasted_iota(jnp.int32, (cols, mixed.shape[1]), 0)
    for r in range(rows):
        part = slice(r * cols, (r + 1) * cols)
        inner = inner_ref[part].astype(F32)
        inner = jnp.where(sub == 0, mixed[r : r + 1], inner)
        inner = jnp.where(sub == cols - 1, mixed[rows + r : rows + r + 1], inner)
        mixed_ref[part] = inner.astype(BF16)
    pairs = cols // 2
    strips = rows // 2
    for s in range(strips):
        for side, c2 in ((0, 0), (1, pairs - 1)):
            k = s * pairs + c2
            old = sent_ref[k].astype(F32)
            keep = [old[0:1], old[1:2], old[2:3], old[3:4]]
            for m in range(2):
                at = side * rows + m * strips + s
                keep[2 * m + side] = normed[at : at + 1]
            out_ref[k] = jnp.concatenate(keep, axis=0).astype(BF16)


def attend_kernel(x_ref, w_ref, bias_ref, out_ref, x_buf, qk_buf, v_buf, s_buf, p_buf, t_buf, *, heads):
    tokens = 4 * x_ref.shape[0]
    width = x_ref.shape[2]
    head_dim = width // heads
    for k in range(tokens // 4):
        x_buf[4 * k : 4 * k + 4, :] = x_ref[k].astype(F32)
    x = x_buf[...].astype(BF16)
    scale = np.float32(head_dim**-0.5) * LOG2E
    per = 128 // head_dim
    wide = 256
    row_head = lax.broadcasted_iota(jnp.int32, (128, tokens), 0) // head_dim
    ones = jnp.ones((16, tokens), BF16)

    def packs(g):
        return range(g * wide // 128, (g + 1) * wide // 128)

    def span(p):
        return slice(per * tokens * p, per * tokens * (p + 1))

    def project(g):
        for i, ref, at in ((0, qk_buf, 0), (1, qk_buf, width), (2, v_buf, 0)):
            lanes = slice(wide * g, wide * (g + 1))
            w = w_ref[:, i * width + lanes.start : i * width + lanes.stop]
            ref[:, at + lanes.start : at + lanes.stop] = jnp.dot(
                x, w, preferred_element_type=F32
            ).astype(BF16)

    def score(g):
        for p in packs(g):
            q = jnp.transpose(qk_buf[:, 128 * p : 128 * (p + 1)])
            queries = jnp.concatenate(
                [jnp.where(row_head == j, q, jnp.zeros_like(q)) for j in range(per)], axis=1
            )
            keys = qk_buf[:, width + 128 * p : width + 128 * (p + 1)]
            s_buf[:, span(p)] = jnp.dot(keys, queries, preferred_element_type=F32)

    def weigh(g):
        for h in range(g * wide // head_dim, (g + 1) * wide // head_dim):
            base = bias_ref[h]
            bias = jnp.concatenate(
                [base if n == 0 else pltpu.roll(base, 2 * GRID * n, 1) for n in range(GRID)], axis=0
            )
            lanes = slice(tokens * h, tokens * (h + 1))
            s = s_buf[:, lanes] * scale + bias
            p_buf[:, lanes] = jnp.exp2(s - jnp.max(s, axis=0, keepdims=True)).astype(BF16)

    def gather(g):
        for p in packs(g):
            values = jnp.concatenate(
                [jnp.transpose(v_buf[:, 128 * p : 128 * (p + 1)]), ones], axis=0
            )
            summed = jnp.dot(values, p_buf[:, span(p)], preferred_element_type=F32)
            for j in range(per):
                block = summed[:, tokens * j : tokens * (j + 1)]
                at = 128 * p + head_dim * j
                t_buf[at : at + head_dim, :] = block[head_dim * j : head_dim * (j + 1)] * (
                    1.0 / block[128:129]
                )

    def turn(g):
        for p in packs(g):
            x_buf[:, 128 * p : 128 * (p + 1)] = jnp.transpose(t_buf[128 * p : 128 * (p + 1), :])

    for stage, g in (
        (project, 0), (project, 1), (score, 0), (project, 2), (score, 1), (weigh, 0), (score, 2),
        (weigh, 1), (gather, 0), (weigh, 2), (gather, 1), (turn, 0), (gather, 2), (turn, 1), (turn, 2),
    ):
        stage(g)
    for k in range(tokens // 4):
        out_ref[k] = x_buf[4 * k : 4 * k + 4, :].astype(BF16)


def out_kernel(a_ref, w_ref, mixed_ref, out_ref, a_buf, *, rows, cols):
    strips, pairs = rows // 2, cols // 2
    for k in range(a_ref.shape[0]):
        got = a_ref[k].astype(F32)
        for m in range(2):
            at = (m * strips + k // pairs) * cols + 2 * (k % pairs)
            a_buf[at : at + 2, :] = got[2 * m : 2 * m + 2]
    result = mixed_ref[...].astype(F32) + jnp.dot(
        a_buf[...].astype(BF16), w_ref[...], preferred_element_type=F32
    )
    out_ref[...] = result.astype(BF16)


def local(expanded, stream, land, polar, land_shift, dw_kernel, w_proj, w_qkv, w_out, rel_bias):
    rows, cols, width_exp = expanded.shape
    width = stream.shape[2]
    heads = rel_bias.shape[0]
    tokens = rows * cols
    lon, lat = ("nhi", "nlo"), "lat"
    lons, lats = lax.axis_size(lon), lax.axis_size(lat)
    everyone = lon + (lat,)
    swap_core = [(i, i ^ 1) for i in range(lats)]
    swap_next = [(i, (i + 1) % lats if i % 2 else (i - 1) % lats) for i in range(lats)]

    def call(kernel, name, ins, in_specs, outs, scratch, limit, **more):
        return pl.pallas_call(
            kernel,
            name=name,
            out_shape=tuple(pltpu.VMEM(shape, dtype) for shape, dtype in outs),
            in_specs=in_specs,
            out_specs=(VM,) * len(outs),
            scratch_shapes=scratch,
            compiler_params=pltpu.CompilerParams(vmem_limit_bytes=limit << 20),
            **more,
        )(*ins)

    row_shape, col_shape = ((cols, width_exp), BF16), ((rows, width_exp), BF16)
    end_shape = ((2, width_exp), BF16)
    small = (expanded, dw_kernel, land_shift[None], land)
    e_here, taps, shift, land, *picked = call(
        functools.partial(pick_kernel, lat=lat), "pick", map(in_hbm, small), [HBM] * 4,
        [(x.shape, x.dtype) for x in small] + [end_shape] * 2 + [row_shape] * 2 + [col_shape] * 2,
        [pltpu.SemaphoreType.DMA((4,))], 8,
    )
    rel = jnp.transpose(rel_bias, (1, 2, 0)).reshape(-1, heads)
    chunk = 768
    fixed = (e_here, taps, shift, land, *map(in_hbm, (w_proj, rel, polar, stream)))
    inner_outs = [
        ((tokens, width_exp), BF16), ((2 * rows, width_exp), F32), ((tokens, 128), F32),
        (w_proj.shape, BF16), ((heads, 2 * GRID, 128), F32), (stream.shape, BF16),
    ]
    inner_scratch = [
        pltpu.VMEM(rel.shape, F32), pltpu.SMEM(polar.shape, jnp.int32), pltpu.SemaphoreType.DMA((4,)),
    ]
    end_a, end_b, row_a, row_b, first, last = picked
    far_a = lax.ppermute(end_a, lat, swap_core)
    far_b = lax.ppermute(end_b, lat, swap_next)
    got_a = lax.ppermute(row_a, lat, swap_core)
    got_b = lax.ppermute(row_b, lat, swap_next)

    def pack(column, is_last):
        return call(
            functools.partial(pack_kernel, lat=lat, is_last=is_last), "pack",
            (column, far_a, far_b, taps), [VM] * 4, [col_shape], [], 4,
        )[0]

    rightward = pack(last, True)
    from_left = lax.ppermute(rightward, lon, [(i, (i + 1) % lons) for i in range(lons)])
    *inner, first = call(
        functools.partial(inner_kernel, aliased=2, early=True, chunk=chunk), "inner_early",
        (*fixed, first, rightward), [VM] * 4 + [HBM] * 4 + [VM] * 2,
        inner_outs + [col_shape], inner_scratch, 8, input_output_aliases={8: 6},
    )
    leftward = pack(first, False)
    from_right = lax.ppermute(leftward, lon, [(i, (i - 1) % lons) for i in range(lons)])
    act, edge, land_lanes, w_proj, bias, stream = call(
        functools.partial(inner_kernel, aliased=7, early=False, chunk=chunk), "inner_late",
        (*fixed, *inner, leftward), [VM] * 4 + [HBM] * 4 + [VM] * 7, inner_outs, inner_scratch, 8,
        input_output_aliases={8 + i: i for i in range(6)},
        cost_estimate=pl.CostEstimate(flops=10**9, bytes_accessed=10**6, transcendentals=0),
    )
    token_shape, sent_shape = ((tokens, width), BF16), ((tokens // 4, 4, width), BF16)
    mixed, sent, act, edge, w_qkv, w_out = call(
        functools.partial(mix_kernel, chunk=chunk, lat=lat), "mix",
        (
            e_here, got_a, got_b, taps, shift, land_lanes, w_proj, stream,
            in_hbm(w_qkv), in_hbm(w_out), act, edge,
        ),
        [VM] * 8 + [HBM] * 2 + [VM] * 2,
        [token_shape, sent_shape] + inner_outs[:2] + [(w_qkv.shape, BF16), (w_out.shape, BF16)],
        [
            pltpu.VMEM((tokens, tokens), BF16), pltpu.SemaphoreType.DMA((2,)),
        ],
        8, input_output_aliases={10: 2, 11: 3},
        cost_estimate=pl.CostEstimate(flops=10**9, bytes_accessed=10**6, transcendentals=0),
    )
    mixed, sent = call(
        functools.partial(edge_kernel, chunk=width), "edge",
        (edge, from_left, from_right, w_proj, stream, sent, mixed), [VM] * 7,
        [token_shape, sent_shape], [], 8, input_output_aliases={5: 1, 6: 0},
    )

    group = ("nhi", lat)
    mine = lax.all_to_all(sent, group, 0, 0, tiled=True)
    attended = pl.pallas_call(
        functools.partial(attend_kernel, heads=heads),
        name="attend",
        out_shape=jax.ShapeDtypeStruct((tokens // 4, 4, width), BF16),
        in_specs=[VM] * 3,
        out_specs=VM,
        scratch_shapes=[
            pltpu.VMEM((tokens, width), F32), pltpu.VMEM((tokens, 2 * width), BF16),
            pltpu.VMEM((tokens, width), BF16), pltpu.VMEM((tokens, tokens * heads), F32),
            pltpu.VMEM((tokens, tokens * heads), BF16), pltpu.VMEM((width, tokens), F32),
        ],
        compiler_params=pltpu.CompilerParams(vmem_limit_bytes=8 << 20),
    )(mine, w_qkv, bias)
    back = lax.all_to_all(attended, group, 0, 0, tiled=True)
    result = pl.pallas_call(
        functools.partial(out_kernel, rows=rows, cols=cols),
        name="out",
        out_shape=jax.ShapeDtypeStruct((tokens, width), BF16),
        in_specs=[VM] * 3,
        out_specs=VM,
        scratch_shapes=[pltpu.VMEM((tokens, width), F32)],
        compiler_params=pltpu.CompilerParams(vmem_limit_bytes=8 << 20),
    )(back, w_out, mixed)
    return result.reshape(rows, cols, width)


def solution(mesh):
    lons, lats = mesh.shape["lon"], mesh.shape["lat"]
    fine = Mesh(mesh.devices.reshape(GRID, lons // GRID, lats), ("nhi", "nlo", "lat"))
    lon = ("nhi", "nlo")
    in_specs = (P("lat", lon, None), P("lat", lon, None), P("lat", lon)) + (P(),) * 7
    return jax.shard_map(
        local, mesh=fine, in_specs=in_specs, out_specs=P("lat", lon, None), check_vma=False
    )
```
